128 devices in a mesh: band: 32 (over z_lo, y, x), member: 4 (over z_hi, core).
Axes of the slice: x: 4, y: 4, z: 4 (z_hi: 2, z_lo: 2; z = z_hi * 2 + z_lo), core: 2. Of those that a mesh axis runs over, the one named last changes fastest.
Arguments:
- state_field: bfloat16 [128, 1440, 128], P('band'), may hold values from -6 to 6
- observed_target: bfloat16 [128, 1440, 128], P('band'), may hold values from -6 to 6
- feature_jitter_amplitude: float32 [128], replicated, may hold values from 0.2 to 1
- leading_filter: bfloat16 [3, 3, 128, 128], replicated, may hold values from -0.1875 to 0.1875
- trailing_filter: bfloat16 [3, 3, 128, 128], replicated, may hold values from -0.1875 to 0.1875
- parallels_each_strip: int32 [32], replicated, may hold values from 1 to 4, 96 in all
- realization_random_keys: int32 [4], P('member'), may hold values from 0 to 999999
Outputs:
- crps_cells: float32 [128, 1440], P('band', 'member')
- mean_loss: float32 [], replicated
- grad_one: float32 [3, 3, 128, 128], replicated
- trailing_filter_derivative: float32 [3, 3, 128, 128], replicated
The draws below stay inside these ranges and needn't reach their ends.
Inputs may be any that keep to these rules, and one draw needn't show every extreme that they name: `parallels_each_strip`: each band holds 1 to 4 rows, together 96, and some band holds exactly 4.
All inputs are finite; a program needn't handle non-finite values.
Results may differ from the reference program's by a relative error of at most 0.00075.
The reference program's roundings to bfloat16 on the way count: a program that leaves them out, or rounds other values in their place, can miss the bound.
Values may be sent and summed in bfloat16 or wider, within the bound.
No kernel may reach another device: no remote copies, remote signals or barrier semaphores. Data moves between devices by JAX's collectives and lax.ppermute only.
A program may use at most 128 MiB of HBM per device.

```python
import math
import jax
import jax.numpy as jnp
import numpy as np
from jax import lax

ROWS_MAX = 4
EASTWARD_POINTS = 1440
INNER_FEATURES = 128
GRID_ROWS = 721
MEMBERS = 4
ROWS = 128
ROWS_TOTAL = 96
N_BAND = 32
N_MEMBER = 4


def plant(drawn, rng, least, largest):
    spot = [jax.random.randint(jax.random.fold_in(rng, axis), (), 0, length) for axis, length in enumerate(drawn.shape)]
    longest = drawn.shape.index(max(drawn.shape))
    neighbour = spot[:longest] + [(spot[longest] + 1) % drawn.shape[longest]] + spot[longest + 1:]
    return drawn.at[tuple(spot)].set(least).at[tuple(neighbour)].set(largest)


def shard_levels(own_key, dims, cuts, least, largest):
    loudness, own = 1.0, jax.random.fold_in(own_key, 6)
    for position, blocks in cuts:
        draws = jnp.exp(jax.random.uniform(jax.random.fold_in(own, position), (blocks,), jnp.float32, least / len(cuts), largest / len(cuts)))
        loudness = loudness * jnp.repeat(draws, dims[position] // blocks).reshape([-1 if axis == position else 1 for axis in range(len(dims))])
    return loudness


def length_profile(number_of, total, bound, lean):
    weights = [(1 << 20) // math.isqrt(standing ** lean) + 1 for standing in range(2, number_of + 1)]
    rest, holding = total - bound - (number_of - 1), [1] * (number_of - 1)
    while rest > 0:
        free = [i for i in range(number_of - 1) if holding[i] < bound]
        pool, budget = sum([weights[i] for i in free]), rest
        for i in free:
            addition = min(bound - holding[i], max(1, budget * weights[i] // pool), rest)
            holding[i] = holding[i] + addition
            rest = rest - addition
    return np.array([bound] + holding)


def uneven(rng, amount, total, most, lean):
    if amount == 2:
        one = jax.random.randint(rng, (), max(1, total - most), min(most, total - 1) + 1)
        return jnp.stack([one, total - one])
    tallies = jnp.asarray(length_profile(amount, total, most, lean), jnp.int32)
    pairs = (amount - 1) // 2
    giver, taker = tallies[1:1 + 2 * pairs:2], tallies[2:2 + 2 * pairs:2]
    room = jnp.minimum(giver - 1, most - taker)
    moved = jax.random.randint(jax.random.fold_in(rng, 1), (pairs,), 0, 1 << 20) % (room + 1)
    tallies = tallies.at[1:1 + 2 * pairs:2].set(giver - moved).at[2:2 + 2 * pairs:2].set(taker + moved)
    return tallies[jax.random.permutation(jax.random.fold_in(rng, 2), amount)]


def noise(rng, shape, scale, reach, cuts=(), held_as=jnp.bfloat16):
    factor_of = shard_levels(rng, shape, cuts, -0.22, 0.18) if cuts else 1.0
    array = jax.random.normal(rng, shape, jnp.float32) * scale * factor_of
    return jnp.minimum(jnp.maximum(array, -reach), reach).astype(held_as)


def setup_inputs(seed: int = 0) -> dict:
    arg_keys = jax.random.split(jax.random.key(seed), 8)
    state_field = noise(arg_keys[0], (ROWS, EASTWARD_POINTS, INNER_FEATURES), 1.0, 6.0, ((0, 32),))
    observed_target = noise(arg_keys[1], (ROWS, EASTWARD_POINTS, INNER_FEATURES), 1.0, 6.0, ((0, 32),))
    feature_jitter_amplitude = jnp.clip(jnp.exp(jax.random.uniform(arg_keys[2], (INNER_FEATURES,), jnp.float32, math.log(0.2), math.log(1.0))), 0.2, 1.0)
    leading_filter = noise(arg_keys[3], (3, 3, INNER_FEATURES, INNER_FEATURES), (9 * INNER_FEATURES) ** -0.5, 0.1875)
    trailing_filter = noise(arg_keys[4], (3, 3, INNER_FEATURES, INNER_FEATURES), (9 * INNER_FEATURES) ** -0.5, 0.1875)
    parallels_each_strip = uneven(arg_keys[5], N_BAND, ROWS_TOTAL, ROWS_MAX, 2).astype(jnp.int32)
    realization_random_keys = plant(jax.random.randint(arg_keys[6], (MEMBERS,), 0, 1000000), jax.random.fold_in(arg_keys[6], 1), 0, 999999).astype(jnp.int32)
    return dict(state_field=state_field, observed_target=observed_target, feature_jitter_amplitude=feature_jitter_amplitude, leading_filter=leading_filter, trailing_filter=trailing_filter, parallels_each_strip=parallels_each_strip, realization_random_keys=realization_random_keys)


smooth_sq = 0.01

def cell_noise(seed_value, first_row, strip_depth, meridian_entries, channels):
    global_row = first_row.astype(jnp.int32) + jnp.arange(strip_depth, dtype=jnp.int32)
    col_ids = jnp.arange(meridian_entries, dtype=jnp.int32)
    chan_ids = jnp.arange(channels, dtype=jnp.int32)
    hashed = global_row[:, None, None] * 374761393 + col_ids[None, :, None] * 668265263
    hashed = hashed + chan_ids[None, None, :] * 1274126177 + seed_value.astype(jnp.int32) * 1103515245
    hashed = hashed ^ hashed >> 13
    hashed = hashed * 1274126177
    hashed = hashed ^ hashed >> 16
    return ((hashed & 65535).astype(jnp.float32) + 0.5) / 32768.0 - 1.0

def extend_band_rows(field, upper_row, lower_row, padded_parallels):
    zero_row = jnp.zeros_like(upper_row)
    padded = jnp.concatenate([upper_row[None], field, zero_row[None]], axis=0)
    padded = lax.dynamic_update_slice(padded, lower_row[None], (padded_parallels.astype(jnp.int32) + 1, jnp.int32(0), jnp.int32(0)))
    return jnp.concatenate([padded[:, -1:], padded, padded[:, :1]], axis=1)

def patch_rows(padded, strip_depth, meridian_entries):
    pieces = [padded[shift_row:shift_row + strip_depth, shift_col:shift_col + meridian_entries] for shift_row in range(3) for shift_col in range(3)]
    joined = jnp.concatenate(pieces, axis=2)
    return joined.reshape(strip_depth * meridian_entries, joined.shape[2])

def apply_taps(padded, kernel, strip_depth, meridian_entries):
    channels = kernel.shape[3]
    result = jnp.dot(patch_rows(padded, strip_depth, meridian_entries), kernel.reshape(9 * kernel.shape[2], channels), preferred_element_type=jnp.float32)
    return result.reshape(strip_depth, meridian_entries, channels)

def kernel_weight_gradient(padded, cotangent, strip_depth, meridian_entries):
    patches = patch_rows(padded, strip_depth, meridian_entries)
    flat = cotangent.reshape(strip_depth * meridian_entries, cotangent.shape[2])
    result = lax.dot_general(patches, flat, (((0,), (0,)), ((), ())), preferred_element_type=jnp.float32)
    return result.reshape(3, 3, flat.shape[1], flat.shape[1])

def reversed_filter(kernel):
    return jnp.transpose(kernel[::-1, ::-1], (0, 1, 3, 2))

def silu_slope(linear_response):
    sig = jax.nn.sigmoid(linear_response)
    return sig * (1.0 + linear_response * (1.0 - sig))

def unbiased_crps_parts(realization_prediction, observed_target, filter_coefficient, derivative_factor):
    realization_group = realization_prediction.shape[0]
    target = observed_target.astype(jnp.float32)
    crps_results = [realization_prediction[opening_realization_number].astype(jnp.float32) for opening_realization_number in range(realization_group)]
    skill_sum = jnp.zeros_like(target)
    spread_sum = jnp.zeros_like(target)
    slopes = []
    for opening_realization_number in range(realization_group):
        diff = crps_results[opening_realization_number] - target
        smooth = jnp.sqrt(diff * diff + smooth_sq)
        skill_sum = skill_sum + smooth
        slopes.append(diff / smooth / realization_group)
    pair_scale = 1.0 / (realization_group * (realization_group - 1))
    for opening_realization_number in range(realization_group):
        for index_b in range(opening_realization_number + 1, realization_group):
            diff = crps_results[opening_realization_number] - crps_results[index_b]
            smooth = jnp.sqrt(diff * diff + smooth_sq)
            spread_sum = spread_sum + smooth
            tilt = diff / smooth * pair_scale
            slopes[opening_realization_number] = slopes[opening_realization_number] - tilt
            slopes[index_b] = slopes[index_b] + tilt
    crps = skill_sum / realization_group - spread_sum * pair_scale
    crps_pointwise = lax.optimization_barrier(jnp.mean(crps, axis=-1)) * filter_coefficient[..., 0]
    grand_accumulation = jnp.sum(crps * filter_coefficient)
    filter_derivatives = (jnp.stack(slopes) * (filter_coefficient * derivative_factor)).astype(jnp.bfloat16)
    return (crps_pointwise, grand_accumulation, filter_derivatives)

def neighbours(field, parallels_each_strip):
    parallel_strips = field.shape[0]
    last_rows = field[jnp.arange(parallel_strips), parallels_each_strip - 1]
    zero_row = jnp.zeros_like(field[:1, 0])
    upper = jnp.concatenate([zero_row, last_rows[:-1]], axis=0)
    lower = jnp.concatenate([field[1:, 0], zero_row], axis=0)
    return (upper, lower)

def filter_all_strips(field, parallels_each_strip, kernel):
    upper, lower = neighbours(field, parallels_each_strip)
    strip_depth, meridian_entries = (field.shape[1], field.shape[2])

    def one_band(items):
        piece, upper_row, lower_row, padded_parallels = items
        return apply_taps(extend_band_rows(piece, upper_row, lower_row, padded_parallels), kernel, strip_depth, meridian_entries)
    return lax.map(one_band, (field, upper, lower, parallels_each_strip))

def derivative_all_strips(field, cotangent, parallels_each_strip):
    upper, lower = neighbours(field, parallels_each_strip)
    strip_depth, meridian_entries = (field.shape[1], field.shape[2])

    def one_band(items):
        piece, cot_piece, upper_row, lower_row, padded_parallels = items
        return kernel_weight_gradient(extend_band_rows(piece, upper_row, lower_row, padded_parallels), cot_piece, strip_depth, meridian_entries)
    return lax.optimization_barrier(jnp.sum(lax.map(one_band, (field, cotangent, upper, lower, parallels_each_strip)), axis=0))

def band_masks(parallels_each_strip, strip_depth):
    offsets = (jnp.cumsum(parallels_each_strip) - parallels_each_strip).astype(jnp.int32)
    row_ids = jnp.arange(strip_depth, dtype=jnp.int32)
    genuine_parallel_flags = (row_ids[None, :] < parallels_each_strip[:, None]).astype(jnp.float32)[:, :, None, None]
    return (offsets, row_ids, genuine_parallel_flags)

def evaluate_model(strip_split_field, parallels_each_strip, seed_value, feature_jitter_amplitude, leading_filter, trailing_filter):
    parallel_strips, strip_depth, meridian_entries, channels = strip_split_field.shape
    offsets, row_ids, genuine_parallel_flags = band_masks(parallels_each_strip, strip_depth)
    noise_field = jax.vmap(lambda start: cell_noise(seed_value, start, strip_depth, meridian_entries, channels))(offsets)
    perturbed_source = ((strip_split_field.astype(jnp.float32) + feature_jitter_amplitude * noise_field) * genuine_parallel_flags).astype(jnp.bfloat16)
    linear_response = filter_all_strips(perturbed_source, parallels_each_strip, leading_filter)
    inner_response = (jax.nn.silu(linear_response) * genuine_parallel_flags).astype(jnp.bfloat16)
    realization_prediction = ((perturbed_source.astype(jnp.float32) + filter_all_strips(inner_response, parallels_each_strip, trailing_filter)) * genuine_parallel_flags).astype(jnp.bfloat16)
    return (perturbed_source, linear_response, inner_response, realization_prediction)

def reference(state_field, observed_target, feature_jitter_amplitude, leading_filter, trailing_filter, parallels_each_strip, realization_random_keys):
    parallel_strips = N_BAND
    strip_depth = ROWS_MAX
    parallels_each_strip = parallels_each_strip.astype(jnp.int32)
    strip_split_field = state_field.reshape(parallel_strips, strip_depth, EASTWARD_POINTS, INNER_FEATURES)
    prediction_pile = []
    for single_realization in range(N_MEMBER):
        prediction_pile.append(evaluate_model(strip_split_field, parallels_each_strip, realization_random_keys[single_realization], feature_jitter_amplitude, leading_filter, trailing_filter)[3])
    realization_prediction = jnp.stack(prediction_pile).reshape(N_MEMBER, parallel_strips * strip_depth, EASTWARD_POINTS, INNER_FEATURES)
    offsets, row_ids, genuine_parallel_flags = band_masks(parallels_each_strip, strip_depth)
    global_row = (offsets[:, None] + row_ids[None, :]).astype(jnp.float32)
    latitude = jnp.pi * ((global_row + 0.5) / GRID_ROWS - 0.5)
    filter_coefficient = (jnp.cos(latitude)[:, :, None, None] * genuine_parallel_flags).reshape(parallel_strips * strip_depth, 1, 1)
    derivative_factor = 1.0 / math.sqrt(ROWS_TOTAL * EASTWARD_POINTS)
    crps_pointwise, grand_accumulation, filter_derivatives = unbiased_crps_parts(realization_prediction, observed_target, filter_coefficient, derivative_factor)
    grad_one = jnp.zeros((3, 3, INNER_FEATURES, INNER_FEATURES), jnp.float32)
    trailing_filter_derivative = jnp.zeros((3, 3, INNER_FEATURES, INNER_FEATURES), jnp.float32)
    for single_realization in range(N_MEMBER):
        perturbed_source, linear_response, inner_response, unused = evaluate_model(strip_split_field, parallels_each_strip, realization_random_keys[single_realization], feature_jitter_amplitude, leading_filter, trailing_filter)
        prediction_adjoint = filter_derivatives[single_realization].reshape(parallel_strips, strip_depth, EASTWARD_POINTS, INNER_FEATURES)
        inner_adjoint = filter_all_strips(prediction_adjoint, parallels_each_strip, reversed_filter(trailing_filter))
        pre_cot = (inner_adjoint * silu_slope(linear_response) * genuine_parallel_flags).astype(jnp.bfloat16)
        trailing_filter_derivative = trailing_filter_derivative + derivative_all_strips(inner_response, prediction_adjoint, parallels_each_strip)
        grad_one = grad_one + derivative_all_strips(perturbed_source, pre_cot, parallels_each_strip)
    mean_loss = grand_accumulation / (ROWS_TOTAL * EASTWARD_POINTS * INNER_FEATURES)
    return (crps_pointwise, mean_loss, grad_one, trailing_filter_derivative)
```

```python
import math

import jax
import jax.numpy as jnp
import numpy as np
from jax import lax
from jax.experimental import pallas as pl
from jax.experimental.pallas import tpu as pltpu
from jax.sharding import PartitionSpec as P

GRID_ROWS = 721
ROWS_TOTAL = 96
SMOOTH = 0.01
LON = 1440
OWN = 360
LEFT = 8
J = 384
C = 128
MEM = 4
SLOTS = 4
DEPTH = 3
EXT = SLOTS + 2 * DEPTH
PAD = 8
R = 2368
BF = jnp.bfloat16
F32 = jnp.float32
BM = ("band", "member")


def coords(i):
    return [i // 64, i // 16 % 4, i // 4 % 4, i // 2 % 2, i % 2]


def index(v):
    return (((v[0] * 4 + v[1]) * 4 + v[2]) * 2 + v[3]) * 2 + v[4]


SIZES = [2, 4, 4, 2, 2]


def shift(value, dim, by):
    pairs = []
    for i in range(128):
        v = coords(i)
        v[dim] = (v[dim] + by) % SIZES[dim]
        pairs.append((i, index(v)))
    return lax.ppermute(value, BM, pairs)


def scatter_sum(value, dim, place):
    n = SIZES[dim]
    parts = value.reshape(n, value.shape[0] // n, C)
    total = lax.dynamic_index_in_dim(parts, place, 0, keepdims=False)
    got = [
        shift(lax.dynamic_index_in_dim(parts, (place + d) % n, 0, keepdims=False), dim, d)
        for d in range(1, n)
    ]
    for g in got:
        total = total + g
    return total


def exchange_sum(value, dim):
    got = [shift(value, dim, d) for d in range(1, SIZES[dim])]
    for g in got:
        value = value + g
    return value


def gather(value, dim, place):
    n = SIZES[dim]
    got = [shift(value, dim, d) for d in range(1, n)]
    out = jnp.zeros((n,) + value.shape, value.dtype)
    out = lax.dynamic_update_index_in_dim(out, value, place, 0)
    for d, g in enumerate(got, 1):
        out = lax.dynamic_update_index_in_dim(out, g, (place - d) % n, 0)
    return out.reshape(n * value.shape[0], C)


def sigmoid(a):
    return 1.0 / (1.0 + jnp.exp(-a))


def kernel(
    counts_ref, seeds_ref, place_ref, weight_ref,
    own_ref, fwd1_ref, fwd2_ref, fwd3_ref, bwd1_ref, bwd2_ref, bwd3_ref,
    target_ref, amp_ref, w1_ref, w2_ref, wt_ref,
    grads_ref, cells_ref,
    state_s, tgt_s, hash_s, buf_s, in3_s, hid3_s, cot3_s, pre_s, fc_s, ya_s, yb_s, acc_s,
):
    band = place_ref[0]
    quarter = place_ref[1]
    n = counts_ref[band]

    def count(b):
        inside = (b >= 0) & (b < 32)
        return jnp.where(inside, counts_ref[jnp.clip(b, 0, 31)], 4)

    offset = lax.fori_loop(0, band, lambda b, s: s + counts_ref[b], jnp.int32(0))
    up1, up2 = count(band - 1), count(band - 2)
    dn1, dn2 = count(band + 1), count(band + 2)

    state_s[DEPTH : DEPTH + SLOTS] = own_ref[...]
    state_s[2] = fwd1_ref[2]

    def pick(dst, cond, a, b):
        @pl.when(cond)
        def _():
            state_s[dst] = a()

        @pl.when(jnp.logical_not(cond))
        def _():
            state_s[dst] = b()

    pick(1, up1 >= 2, lambda: fwd1_ref[1], lambda: fwd2_ref[1])
    pick(0, up2 >= 2, lambda: fwd2_ref[0], lambda: fwd3_ref[0])

    @pl.when(up1 == 2)
    def _():
        state_s[0] = fwd2_ref[1]

    @pl.when(up1 >= 3)
    def _():
        state_s[0] = fwd1_ref[0]

    below = DEPTH + n
    state_s[below] = bwd1_ref[0]
    pick(below + 1, dn1 >= 2, lambda: bwd1_ref[1], lambda: bwd2_ref[0])
    pick(below + 2, dn2 >= 2, lambda: bwd2_ref[1], lambda: bwd3_ref[0])

    @pl.when(dn1 == 2)
    def _():
        state_s[below + 2] = bwd2_ref[0]

    @pl.when(dn1 >= 3)
    def _():
        state_s[below + 2] = bwd1_ref[2]

    tgt_s[1 : 1 + SLOTS] = target_ref[...]
    tgt_s[0] = fwd1_ref[3]
    tgt_s[1 + n] = bwd1_ref[3]

    buf_s[0:PAD] = jnp.zeros((PAD, C), F32)
    buf_s[PAD + J :] = jnp.zeros((PAD, C), F32)

    cols = lax.broadcasted_iota(jnp.int32, (J, C), 0)
    chan = lax.broadcasted_iota(jnp.int32, (J, C), 1)
    lon = quarter * OWN - LEFT + cols
    lon = jnp.where(lon < 0, lon + LON, jnp.where(lon >= LON, lon - LON, lon))
    hash_s[...] = lon * 668265263 + chan * 1274126177
    own_col = ((cols >= LEFT) & (cols < LEFT + OWN)).astype(F32)

    def valid(e):
        g = offset - DEPTH + e
        return ((g >= 0) & (g < ROWS_TOTAL)).astype(F32)

    def put3(ref, m, e, v):
        buf_s[PAD : PAD + J] = v
        ref[m, e, :, C : 2 * C] = v.astype(BF)
        ref[m, e, :, 0:C] = buf_s[PAD - 1 : PAD - 1 + J].astype(BF)
        ref[m, e, :, 2 * C :] = buf_s[PAD + 1 : PAD + 1 + J].astype(BF)

    amp = amp_ref[...]

    def make_inputs(i, _):
        e, m = i // MEM, i % MEM
        base = (offset - DEPTH + e) * 374761393 + seeds_ref[m] * 1103515245
        h = hash_s[...] + base
        h = h ^ (h >> 13)
        h = h * 1274126177
        h = h ^ (h >> 16)
        noise = (h & 65535).astype(F32) * (1.0 / 32768.0) + (0.5 / 32768.0 - 1.0)
        v = (state_s[e].astype(F32) + amp * noise) * valid(e)
        put3(in3_s, m, e, v)
        return 0

    lax.fori_loop(0, EXT * MEM, make_inputs, 0)

    def conv_pair(ref, m, e, w):
        lhs = jnp.concatenate([ref[m, e + s] for s in range(4)], axis=1)
        return jnp.dot(lhs, w[...], preferred_element_type=F32)

    def make_hidden(i, _):
        p, m = i // MEM, i % MEM
        out = conv_pair(in3_s, m, 2 * p, w1_ref)
        for k in range(2):
            e = 1 + 2 * p + k
            a = out[:, k * C : (k + 1) * C]

            @pl.when((e >= DEPTH) & (e < DEPTH + SLOTS))
            def _():
                pre_s[m, e - DEPTH] = a

            put3(hid3_s, m, e - 1, a * sigmoid(a) * valid(e))
        return 0

    lax.fori_loop(0, 4 * MEM, make_hidden, 0)

    def make_forecast(i, _):
        p, m = i // MEM, i % MEM
        out = conv_pair(hid3_s, m, 2 * p, w2_ref)
        for k in range(2):
            e = 2 + 2 * p + k
            v = (in3_s[m, e, :, C : 2 * C].astype(F32) + out[:, k * C : (k + 1) * C]) * valid(e)
            fc_s[m, e - 2] = v.astype(BF)
        return 0

    lax.fori_loop(0, 3 * MEM, make_forecast, 0)

    pair_scale = 1.0 / (MEM * (MEM - 1))
    factor = 1.0 / math.sqrt(ROWS_TOTAL * LON)

    def make_crps(r, loss):
        e = r + 2
        g = jnp.clip(offset - DEPTH + e, 0, ROWS_TOTAL - 1)
        weight = weight_ref[g] * valid(e)
        mine = ((r >= 1) & (r < 1 + n)).astype(F32)
        t = tgt_s[r].astype(F32)
        f = [fc_s[m, r].astype(F32) for m in range(MEM)]
        skill = jnp.zeros_like(t)
        spread = jnp.zeros_like(t)
        slopes = []
        for m in range(MEM):
            d = f[m] - t
            q = d * d + SMOOTH
            inv = lax.rsqrt(q)
            skill = skill + q * inv
            slopes.append(d * inv * (1.0 / MEM))
        for a in range(MEM):
            for b in range(a + 1, MEM):
                d = f[a] - f[b]
                q = d * d + SMOOTH
                inv = lax.rsqrt(q)
                spread = spread + q * inv
                tilt = d * inv * pair_scale
                slopes[a] = slopes[a] - tilt
                slopes[b] = slopes[b] + tilt
        crps = skill * (1.0 / MEM) - spread * pair_scale
        for m in range(MEM):
            v = slopes[m] * (weight * factor)
            put3(cot3_s, m, r, v)

            @pl.when((r >= 1) & (r < 1 + SLOTS))
            def _():
                ya_s[m, r - 1] = (v * (own_col * mine)).astype(BF)

        cell = jnp.sum(jnp.transpose(crps), axis=0, keepdims=True) * (weight * mine / C)

        @pl.when((r >= 1) & (r < 1 + SLOTS))
        def _():
            cells_ref[r - 1] = cell

        return loss + cell

    loss = lax.fori_loop(0, SLOTS + 2, make_crps, jnp.zeros((1, J), F32))
    lane = lax.broadcasted_iota(jnp.int32, (1, J), 1)
    loss = jnp.where((lane >= LEFT) & (lane < LEFT + OWN), loss, 0.0)

    def make_pre_cot(i, _):
        p, m = i // MEM, i % MEM
        out = conv_pair(cot3_s, m, 2 * p, wt_ref)
        for k in range(2):
            s = 2 * p + k
            a = pre_s[m, s]
            sig = sigmoid(a)
            mine = (s < n).astype(F32)
            v = out[:, k * C : (k + 1) * C] * (sig * (1.0 + a * (1.0 - sig))) * (own_col * mine)
            yb_s[m, s] = v.astype(BF)
        return 0

    lax.fori_loop(0, 2 * MEM, make_pre_cot, 0)

    def weight_grad(x3, first, y, row0):
        acc_s[...] = jnp.zeros_like(acc_s)

        def step(m, _):
            ys = jnp.concatenate(
                [
                    jnp.concatenate([y[m, 0], y[m, 1]], axis=1),
                    jnp.concatenate([y[m, 2], y[m, 3]], axis=1),
                ],
                axis=0,
            )
            for s in range(4):
                xs = jnp.concatenate([x3[m, first + s], x3[m, first + 2 + s]], axis=0)
                acc_s[:, s * 384 : (s + 1) * 384] += lax.dot_general(
                    ys, xs, (((0,), (0,)), ((), ())), preferred_element_type=F32
                )
            return 0

        lax.fori_loop(0, MEM, step, 0)
        for k in range(9):
            blk = acc_s[0:C, k * C : (k + 1) * C] + acc_s[C:, 384 + k * C : 384 + (k + 1) * C]
            grads_ref[row0 + k * C : row0 + (k + 1) * C] = jnp.transpose(blk)

    weight_grad(in3_s, 2, yb_s, 0)
    weight_grad(hid3_s, 1, ya_s, 1152)
    total = jnp.sum(loss, axis=1, keepdims=True) * (1.0 / (ROWS_TOTAL * LON))
    grads_ref[2304:R] = jnp.broadcast_to(total, (R - 2304, C))


def local_step(counts, seeds, place, weights, own, f1, f2, f3, b1, b2, b3, target, amp, w1, w2, wt):
    smem = pl.BlockSpec(memory_space=pltpu.SMEM)
    vmem = pl.BlockSpec(memory_space=pltpu.VMEM)
    return pl.pallas_call(
        kernel,
        out_shape=(
            jax.ShapeDtypeStruct((R, C), F32),
            jax.ShapeDtypeStruct((SLOTS, 1, J), F32),
        ),
        in_specs=[smem] * 4 + [vmem] * 12,
        out_specs=(vmem, vmem),
        scratch_shapes=[
            pltpu.VMEM((EXT, J, C), BF),
            pltpu.VMEM((SLOTS + 2, J, C), BF),
            pltpu.VMEM((J, C), jnp.int32),
            pltpu.VMEM((J + 2 * PAD, C), F32),
            pltpu.VMEM((MEM, EXT, J, 3 * C), BF),
            pltpu.VMEM((MEM, EXT - 2, J, 3 * C), BF),
            pltpu.VMEM((MEM, EXT - 4, J, 3 * C), BF),
            pltpu.VMEM((MEM, SLOTS, J, C), F32),
            pltpu.VMEM((MEM, EXT - 4, J, C), BF),
            pltpu.VMEM((MEM, SLOTS, J, C), BF),
            pltpu.VMEM((MEM, SLOTS, J, C), BF),
            pltpu.VMEM((2 * C, 4 * 384), F32),
        ],
        compiler_params=pltpu.CompilerParams(vmem_limit_bytes=60 * 1024 * 1024),
        name="ensemble_step",
    )(counts, seeds, place, weights, own, f1, f2, f3, b1, b2, b3, target, amp, w1, w2, wt)


def paired(filt):
    flat = filt.reshape(9 * C, C)
    return jnp.concatenate(
        [jnp.pad(flat, ((0, 3 * C), (0, 0))), jnp.pad(flat, ((3 * C, 0), (0, 0)))], axis=1
    )


def window(field, start):
    wide = jnp.concatenate([field[:, LON - LEFT :], field, field[:, : J - OWN - LEFT]], axis=1)
    return lax.dynamic_slice_in_dim(wide, start, J, 1)


def body(state, target, amp, filt1, filt2, counts, seed):
    band = lax.axis_index("band")
    member = lax.axis_index("member")
    n = counts[band]
    x = band % 4
    core = member % 2
    weights = jnp.asarray(
        np.cos(np.pi * ((np.arange(ROWS_TOTAL) + 0.5) / GRID_ROWS - 0.5)).astype(np.float32)
    )
    seeds = jnp.where(jnp.arange(MEM) == member, seed, 0)
    seeds = seeds + shift(seeds, 4, 1)
    seeds = seeds + shift(seeds, 3, 1)

    own = window(state, member * OWN)
    tgt = window(target, member * OWN)

    def send(value, by):
        pairs = [(i, i + by) for i in range(32) if 0 <= i + by < 32]
        return lax.ppermute(value, "band", pairs)

    padded = jnp.concatenate([jnp.zeros((3, J, C), BF), own], axis=0)
    last3 = lax.dynamic_slice_in_dim(padded, n, 3, 0)
    last_t = lax.dynamic_slice_in_dim(tgt, n - 1, 1, 0)
    f1 = send(jnp.concatenate([last3, last_t], axis=0), 1)
    b1 = send(jnp.concatenate([own[:3], tgt[:1]], axis=0), -1)
    f2 = send(last3[1:], 2)
    b2 = send(own[:2], -2)
    f3 = send(last3[2:], 3)
    b3 = send(own[:1], -3)

    w1 = paired(filt1)
    w2 = paired(filt2)
    wt = paired(jnp.transpose(filt2[::-1, ::-1], (0, 1, 3, 2)))
    place = jnp.stack([band, member]).astype(jnp.int32)
    grads, cells = local_step(
        counts, seeds, place, weights, own, f1, f2, f3, b1, b2, b3, tgt, amp[None], w1, w2, wt
    )

    part = scatter_sum(grads, 4, core)
    part = scatter_sum(part, 2, x)
    part = exchange_sum(part, 1)
    part = exchange_sum(part, 3)
    part = exchange_sum(part, 0)
    part = gather(part, 2, x)
    full = gather(part, 4, core)

    return (
        cells[:, 0, LEFT : LEFT + OWN],
        full[2304, 0],
        full[:1152].reshape(3, 3, C, C),
        full[1152:2304].reshape(3, 3, C, C),
    )


def solution(mesh):
    in_specs = (P("band", None, None), P("band", None, None), P(), P(), P(), P(), P("member"))
    out_specs = (P("band", "member"), P(), P(), P())
    return jax.shard_map(body, mesh=mesh, in_specs=in_specs, out_specs=out_specs, check_vma=False)
```

```python
import math

import jax
import jax.numpy as jnp
import numpy as np
from jax import lax
from jax.experimental import pallas as pl
from jax.experimental.pallas import tpu as pltpu
from jax.sharding import PartitionSpec as P

GRID_ROWS = 721
HALF = 720
ROWS_TOTAL = 96
SMOOTH = 0.01
LON = 1440
OWN = 360
LEFT = 8
J = 384
C = 128
MEM = 4
SLOTS = 4
DEPTH = 3
EXT = SLOTS + 2 * DEPTH
PAD = 8
W = 752
R = 2368
BF = jnp.bfloat16
F32 = jnp.float32
BM = ("band", "member")


def coords(i):
    return [i // 64, i // 16 % 4, i // 4 % 4, i // 2 % 2, i % 2]


def index(v):
    return (((v[0] * 4 + v[1]) * 4 + v[2]) * 2 + v[3]) * 2 + v[4]


SIZES = [2, 4, 4, 2, 2]


def shift(value, dim, by):
    pairs = []
    for i in range(128):
        v = coords(i)
        v[dim] = (v[dim] + by) % SIZES[dim]
        pairs.append((i, index(v)))
    return lax.ppermute(value, BM, pairs)


def scatter_sum(value, dim, place):
    n = SIZES[dim]
    parts = value.reshape(n, value.shape[0] // n, C)
    total = lax.dynamic_index_in_dim(parts, place, 0, keepdims=False)
    got = [
        shift(lax.dynamic_index_in_dim(parts, (place + d) % n, 0, keepdims=False), dim, d)
        for d in range(1, n)
    ]
    for g in got:
        total = total + g
    return total


def exchange_sum(value, dim):
    got = [shift(value, dim, d) for d in range(1, SIZES[dim])]
    for g in got:
        value = value + g
    return value


def gather(value, dim, place):
    n = SIZES[dim]
    got = [shift(value, dim, d) for d in range(1, n)]
    out = jnp.zeros((n,) + value.shape, value.dtype)
    out = lax.dynamic_update_index_in_dim(out, value, place, 0)
    for d, g in enumerate(got, 1):
        out = lax.dynamic_update_index_in_dim(out, g, (place - d) % n, 0)
    return out.reshape(n * value.shape[0], C)


def sigmoid(a):
    return 0.5 * jnp.tanh(0.5 * a) + 0.5


def chip_row(half, src, r, dst, sem):
    cut = LON - (HALF - LEFT)
    left = [
        pltpu.make_async_copy(src.at[r, pl.ds(LON - LEFT, LEFT)], dst.at[pl.ds(0, LEFT)], sem.at[0]),
        pltpu.make_async_copy(
            src.at[r, pl.ds(0, W - LEFT)], dst.at[pl.ds(LEFT, W - LEFT)], sem.at[1]
        ),
    ]
    right = [
        pltpu.make_async_copy(src.at[r, pl.ds(HALF - LEFT, cut)], dst.at[pl.ds(0, cut)], sem.at[0]),
        pltpu.make_async_copy(src.at[r, pl.ds(0, W - cut)], dst.at[pl.ds(cut, W - cut)], sem.at[1]),
    ]
    return [(half == 0, left), (half == 1, right)]


def own_window(quarter, src, dst, sem):
    cut = LON - (3 * OWN - LEFT)
    middle = pl.multiple_of(quarter * OWN - LEFT, 8)
    first = [
        pltpu.make_async_copy(
            src.at[:, pl.ds(LON - LEFT, LEFT)], dst.at[:, pl.ds(0, LEFT)], sem.at[0]
        ),
        pltpu.make_async_copy(
            src.at[:, pl.ds(0, J - LEFT)], dst.at[:, pl.ds(LEFT, J - LEFT)], sem.at[1]
        ),
    ]
    inner = [pltpu.make_async_copy(src.at[:, pl.ds(middle, J)], dst, sem.at[0])]
    last = [
        pltpu.make_async_copy(
            src.at[:, pl.ds(3 * OWN - LEFT, cut)], dst.at[:, pl.ds(0, cut)], sem.at[0]
        ),
        pltpu.make_async_copy(
            src.at[:, pl.ds(0, J - cut)], dst.at[:, pl.ds(cut, J - cut)], sem.at[1]
        ),
    ]
    return [(quarter == 0, first), ((quarter == 1) | (quarter == 2), inner), (quarter == 3, last)]


def start(cases):
    for cond, copies in cases:

        @pl.when(cond)
        def _():
            for c in copies:
                c.start()


def wait(cases):
    for cond, copies in cases:

        @pl.when(cond)
        def _():
            for c in copies:
                c.wait()


def edge_kernel(counts_ref, place_ref, state_ref, target_ref, send_ref, second_ref, third_ref, flag_ref, sem):
    n = counts_ref[place_ref[0]]
    member = place_ref[1]
    half, core = member // 2, member % 2
    row = lambda k: jnp.where(core == 0, jnp.maximum(n - 1 - k, 0), k)
    cases = (
        chip_row(half, state_ref, row(0), send_ref.at[0], sem.at[0])
        + chip_row(half, target_ref, row(0), send_ref.at[1], sem.at[1])
        + chip_row(half, state_ref, row(1), second_ref.at[0], sem.at[2])
        + chip_row(half, state_ref, row(2), third_ref.at[0], sem.at[3])
    )
    start(cases)
    ones = jnp.ones((1, C), F32)
    flag_ref[0:1] = ones * (n >= 2).astype(F32)
    flag_ref[1:2] = ones * (n >= 3).astype(F32)
    flag_ref[2:3] = ones * (n == 2).astype(F32)
    flag_ref[3:8] = jnp.zeros((5, C), F32)
    wait(cases)


def edges(counts, place, state, target):
    smem = pl.BlockSpec(memory_space=pltpu.SMEM)
    vmem = pl.BlockSpec(memory_space=pltpu.VMEM)
    hbm = pl.BlockSpec(memory_space=pl.ANY)
    row = jax.ShapeDtypeStruct((1, W, C), BF)
    return pl.pallas_call(
        edge_kernel,
        out_shape=(jax.ShapeDtypeStruct((2, W, C), BF), row, row, jax.ShapeDtypeStruct((8, C), F32)),
        in_specs=[smem, smem, hbm, hbm],
        out_specs=(vmem,) * 4,
        scratch_shapes=[pltpu.SemaphoreType.DMA((4, 2))],
        name="edge_rows",
    )(counts, place, state, target)


def kernel(
    counts_ref, seeds_ref, place_ref, weight_ref,
    state_ref, target_ref, r1_ref, r2_ref, r3_ref, other_ref,
    amp_ref, w1_ref, w2_ref, wt_ref,
    grads_ref, cells_ref,
    state_s, tgt_s, mine_s, hash_s, buf_s, cbuf_s, crps_s,
    in3_s, hid3_s, cot3_s, pre_s, fc_s, ya_s, yb_s, acc_s, sem,
):
    band = place_ref[0]
    quarter = place_ref[1]
    core = quarter % 2
    n = counts_ref[band]
    offset = lax.fori_loop(0, band, lambda b, s: s + counts_ref[b], jnp.int32(0))

    copies = own_window(quarter, state_ref, state_s.at[pl.ds(DEPTH, SLOTS)], sem.at[0])
    copies += own_window(quarter, target_ref, tgt_s.at[pl.ds(1, SLOTS)], sem.at[1])
    lane0 = pl.multiple_of(core * OWN, 8)
    near = [
        pltpu.make_async_copy(r1_ref.at[:, pl.ds(lane0, J)], mine_s.at[pl.ds(0, 2)], sem.at[2, 0]),
        pltpu.make_async_copy(r2_ref.at[:, pl.ds(lane0, J)], mine_s.at[pl.ds(2, 1)], sem.at[2, 1]),
        pltpu.make_async_copy(r3_ref.at[:, pl.ds(lane0, J)], mine_s.at[pl.ds(3, 1)], sem.at[3, 0]),
    ]
    start(copies)
    for c in near:
        c.start()

    buf_s[0:PAD] = jnp.zeros((PAD, C), F32)
    buf_s[PAD + J :] = jnp.zeros((PAD, C), F32)

    cols = lax.broadcasted_iota(jnp.int32, (J, C), 0)
    chan = lax.broadcasted_iota(jnp.int32, (J, C), 1)
    lon = quarter * OWN - LEFT + cols
    lon = jnp.where(lon < 0, lon + LON, jnp.where(lon >= LON, lon - LON, lon))
    hash_s[...] = lon * 668265263 + chan * 1274126177
    own_col = ((cols >= LEFT) & (cols < LEFT + OWN)).astype(F32)

    wait(copies)
    for c in near:
        c.wait()

    def put_edges(above, below):
        for slot, k in ((2, 0), (1, 2), (0, 3)):
            state_s[slot] = above[k]
        for slot, k in ((0, 0), (1, 2), (2, 3)):
            state_s[DEPTH + n + slot] = below[k]
        tgt_s[0] = above[1]
        tgt_s[1 + n] = below[1]

    @pl.when(core == 0)
    def _():
        put_edges(mine_s, other_ref)

    @pl.when(core == 1)
    def _():
        put_edges(other_ref, mine_s)

    def valid(e):
        g = offset - DEPTH + e
        return ((g >= 0) & (g < ROWS_TOTAL)).astype(F32)

    def put3(ref, m, e, v):
        buf_s[PAD : PAD + J] = v
        ref[m, e, :, C : 2 * C] = v.astype(BF)
        ref[m, e, :, 0:C] = buf_s[PAD - 1 : PAD - 1 + J].astype(BF)
        ref[m, e, :, 2 * C :] = buf_s[PAD + 1 : PAD + 1 + J].astype(BF)

    amp = amp_ref[...]

    amp_step = amp * (1.0 / 32768.0)
    amp_base = amp * (0.5 / 32768.0 - 1.0)

    def make_inputs(i, _):
        e, m = i // MEM, i % MEM
        g = offset - DEPTH + e
        inside = (g >= 0) & (g < ROWS_TOTAL)

        @pl.when(inside)
        def _():
            h = hash_s[...] + (g * 374761393 + seeds_ref[m] * 1103515245)
            h = h ^ (h >> 13)
            h = h * 1274126177
            h = h ^ (h >> 16)
            v = (state_s[e].astype(F32) + amp_base) + (h & 65535).astype(F32) * amp_step
            put3(in3_s, m, e, v)

        @pl.when(jnp.logical_not(inside))
        def _():
            in3_s[m, e] = jnp.zeros((J, 3 * C), BF)

        return 0

    lax.fori_loop(0, EXT * MEM, make_inputs, 0)

    def conv_pair(ref, m, e, w):
        lhs = jnp.concatenate([ref[m, e + s] for s in range(4)], axis=1)
        return jnp.dot(lhs, w[...], preferred_element_type=F32)

    def make_hidden(i, _):
        p, m = i // MEM, i % MEM
        out = conv_pair(in3_s, m, 2 * p, w1_ref)
        for k in range(2):
            e = 1 + 2 * p + k
            a = out[:, k * C : (k + 1) * C]

            @pl.when((e >= DEPTH) & (e < DEPTH + SLOTS))
            def _():
                pre_s[m, e - DEPTH] = a

            put3(hid3_s, m, e - 1, a * sigmoid(a) * valid(e))
        return 0

    lax.fori_loop(0, 4 * MEM, make_hidden, 0)

    def make_forecast(i, _):
        p, m = i // MEM, i % MEM
        out = conv_pair(hid3_s, m, 2 * p, w2_ref)
        for k in range(2):
            e = 2 + 2 * p + k
            v = (in3_s[m, e, :, C : 2 * C].astype(F32) + out[:, k * C : (k + 1) * C]) * valid(e)
            fc_s[m, e - 2] = v.astype(BF)
        return 0

    lax.fori_loop(0, 3 * MEM, make_forecast, 0)

    pair_scale = 1.0 / (MEM * (MEM - 1))
    factor = 1.0 / math.sqrt(ROWS_TOTAL * LON)

    step = 32

    def make_crps(r, loss):
        e = r + 2
        g = jnp.clip(offset - DEPTH + e, 0, ROWS_TOTAL - 1)
        weight = weight_ref[g] * valid(e)
        mine = ((r >= 1) & (r < 1 + n)).astype(F32)
        scale = weight * (factor * pair_scale)
        slot = jnp.clip(r - 1, 0, SLOTS - 1)

        def chunk(k, _):
            at = pl.ds(pl.multiple_of(k * step, step), step)
            t = tgt_s[r, at].astype(F32)
            f = [fc_s[m, r, at].astype(F32) for m in range(MEM)]
            skill = None
            spread = None
            slopes = []
            for m in range(MEM):
                d = f[m] - t
                q = d * d + SMOOTH
                inv = lax.rsqrt(q)
                skill = q * inv if skill is None else skill + q * inv
                slopes.append(d * inv * (MEM - 1.0))
            for a in range(MEM):
                for b in range(a + 1, MEM):
                    d = f[a] - f[b]
                    q = d * d + SMOOTH
                    inv = lax.rsqrt(q)
                    spread = q * inv if spread is None else spread + q * inv
                    tilt = d * inv
                    slopes[a] = slopes[a] - tilt
                    slopes[b] = slopes[b] + tilt
            crps_s[at] = (skill * (MEM - 1.0) - spread) * pair_scale
            for m in range(MEM):
                cbuf_s[m, pl.ds(pl.multiple_of(PAD + k * step, 8), step)] = slopes[m] * scale
            return 0

        lax.fori_loop(0, J // step, chunk, 0)
        for m in range(MEM):
            mid = cbuf_s[m, PAD : PAD + J]
            cot3_s[m, r, :, C : 2 * C] = mid.astype(BF)
            cot3_s[m, r, :, 0:C] = cbuf_s[m, PAD - 1 : PAD - 1 + J].astype(BF)
            cot3_s[m, r, :, 2 * C :] = cbuf_s[m, PAD + 1 : PAD + 1 + J].astype(BF)

        @pl.when((r >= 1) & (r < 1 + SLOTS))
        def _():
            for m in range(MEM):
                ya_s[m, slot] = (cbuf_s[m, PAD : PAD + J] * (own_col * mine)).astype(BF)
            cells_ref[slot] = jnp.sum(jnp.transpose(crps_s[...]), axis=0, keepdims=True) * (
                weight * mine * (1.0 / C)
            )

        return loss

    for m in range(MEM):
        cbuf_s[m, 0:PAD] = jnp.zeros((PAD, C), F32)
        cbuf_s[m, PAD + J :] = jnp.zeros((PAD, C), F32)
    lax.fori_loop(0, SLOTS + 2, make_crps, 0)
    loss = cells_ref[0] + cells_ref[1] + cells_ref[2] + cells_ref[3]
    lane = lax.broadcasted_iota(jnp.int32, (1, J), 1)
    loss = jnp.where((lane >= LEFT) & (lane < LEFT + OWN), loss, 0.0)

    def make_pre_cot(i, _):
        p, m = i // MEM, i % MEM
        out = conv_pair(cot3_s, m, 2 * p, wt_ref)
        for k in range(2):
            s = 2 * p + k
            a = pre_s[m, s]
            sig = sigmoid(a)
            mine = (s < n).astype(F32)
            v = out[:, k * C : (k + 1) * C] * (sig * (1.0 + a * (1.0 - sig))) * (own_col * mine)
            yb_s[m, s] = v.astype(BF)
        return 0

    lax.fori_loop(0, 2 * MEM, make_pre_cot, 0)

    def weight_grad(x3, first, y, row0):
        acc_s[...] = jnp.zeros_like(acc_s)

        def step(m, _):
            ys = jnp.concatenate(
                [
                    jnp.concatenate([y[m, 0], y[m, 1]], axis=1),
                    jnp.concatenate([y[m, 2], y[m, 3]], axis=1),
                ],
                axis=0,
            )
            for s in range(4):
                xs = jnp.concatenate([x3[m, first + s], x3[m, first + 2 + s]], axis=0)
                acc_s[:, s * 384 : (s + 1) * 384] += lax.dot_general(
                    ys, xs, (((0,), (0,)), ((), ())), preferred_element_type=F32
                )
            return 0

        lax.fori_loop(0, MEM, step, 0)
        for k in range(9):
            blk = acc_s[0:C, k * C : (k + 1) * C] + acc_s[C:, 384 + k * C : 384 + (k + 1) * C]
            grads_ref[row0 + k * C : row0 + (k + 1) * C] = jnp.transpose(blk)

    weight_grad(in3_s, 2, yb_s, 0)
    weight_grad(hid3_s, 1, ya_s, 1152)
    total = jnp.sum(loss, axis=1, keepdims=True) * (1.0 / (ROWS_TOTAL * LON))
    grads_ref[2304:R] = jnp.broadcast_to(total, (R - 2304, C))


def local_step(counts, seeds, place, weights, state, target, r1, r2, r3, other, amp, w1, w2, wt):
    smem = pl.BlockSpec(memory_space=pltpu.SMEM)
    vmem = pl.BlockSpec(memory_space=pltpu.VMEM)
    hbm = pl.BlockSpec(memory_space=pl.ANY)
    return pl.pallas_call(
        kernel,
        out_shape=(
            jax.ShapeDtypeStruct((R, C), F32),
            jax.ShapeDtypeStruct((SLOTS, 1, J), F32),
        ),
        in_specs=[smem] * 4 + [hbm] * 5 + [vmem] * 5,
        out_specs=(vmem, vmem),
        scratch_shapes=[
            pltpu.VMEM((EXT, J, C), BF),
            pltpu.VMEM((SLOTS + 2, J, C), BF),
            pltpu.VMEM((4, J, C), BF),
            pltpu.VMEM((J, C), jnp.int32),
            pltpu.VMEM((J + 2 * PAD, C), F32),
            pltpu.VMEM((MEM, J + 2 * PAD, C), F32),
            pltpu.VMEM((J, C), F32),
            pltpu.VMEM((MEM, EXT, J, 3 * C), BF),
            pltpu.VMEM((MEM, EXT - 2, J, 3 * C), BF),
            pltpu.VMEM((MEM, EXT - 4, J, 3 * C), BF),
            pltpu.VMEM((MEM, SLOTS, J, C), F32),
            pltpu.VMEM((MEM, EXT - 4, J, C), BF),
            pltpu.VMEM((MEM, SLOTS, J, C), BF),
            pltpu.VMEM((MEM, SLOTS, J, C), BF),
            pltpu.VMEM((2 * C, 4 * 384), F32),
            pltpu.SemaphoreType.DMA((4, 2)),
        ],
        compiler_params=pltpu.CompilerParams(vmem_limit_bytes=60 * 1024 * 1024),
        name="ensemble_step",
    )(counts, seeds, place, weights, state, target, r1, r2, r3, other, amp, w1, w2, wt)


def paired(filt):
    flat = filt.reshape(9 * C, C)
    return jnp.concatenate(
        [jnp.pad(flat, ((0, 3 * C), (0, 0))), jnp.pad(flat, ((3 * C, 0), (0, 0)))], axis=1
    )


def body(state, target, amp, filt1, filt2, counts, seed):
    band = lax.axis_index("band")
    member = lax.axis_index("member")
    x = band % 4
    core = member % 2
    weights = jnp.asarray(
        np.cos(np.pi * ((np.arange(ROWS_TOTAL) + 0.5) / GRID_ROWS - 0.5)).astype(np.float32)
    )
    seeds = jnp.where(jnp.arange(MEM) == member, seed, 0)
    seeds = seeds + shift(seeds, 4, 1)
    seeds = seeds + shift(seeds, 3, 1)

    place = jnp.stack([band, member]).astype(jnp.int32)
    send, second, third, flags = edges(counts, place, state, target)

    pairs = []
    for i in range(128):
        b, core_of = i // 4, i % 2
        to = b + 1 - 2 * core_of
        if 0 <= to < 32:
            pairs.append((i, to * 4 + i % 4))

    def relay(value):
        return lax.ppermute(value, BM, pairs)

    def flag(k):
        return flags[k : k + 1][None] > 0.5

    r1 = relay(send)
    r2 = relay(jnp.where(flag(0), second, r1[:1]))
    r3 = relay(jnp.where(flag(1), third, jnp.where(flag(2), r1[:1], r2)))
    other = shift(
        lax.dynamic_slice_in_dim(jnp.concatenate([r1, r2, r3], axis=0), OWN * (1 - core), J, 1), 4, 1
    )

    w1 = paired(filt1)
    w2 = paired(filt2)
    wt = paired(jnp.transpose(filt2[::-1, ::-1], (0, 1, 3, 2)))
    grads, cells = local_step(
        counts, seeds, place, weights, state, target, r1, r2, r3, other, amp[None], w1, w2, wt
    )

    part = scatter_sum(grads, 4, core)
    part = scatter_sum(part, 2, x)
    part = exchange_sum(part, 1)
    part = exchange_sum(part, 3)
    part = exchange_sum(part, 0)
    part = gather(part, 2, x)
    full = gather(part, 4, core)

    return (
        cells[:, 0, LEFT : LEFT + OWN],
        full[2304, 0],
        full[:1152].reshape(3, 3, C, C),
        full[1152:2304].reshape(3, 3, C, C),
    )


def solution(mesh):
    in_specs = (P("band", None, None), P("band", None, None), P(), P(), P(), P(), P("member"))
    out_specs = (P("band", "member"), P(), P(), P())
    return jax.shard_map(body, mesh=mesh, in_specs=in_specs, out_specs=out_specs, check_vma=False)
```

```python
import math

import jax
import jax.numpy as jnp
import numpy as np
from jax import lax
from jax.experimental import pallas as pl
from jax.experimental.pallas import tpu as pltpu
from jax.sharding import PartitionSpec as P

GRID_ROWS = 721
HALF = 720
ROWS_TOTAL = 96
SMOOTH = 0.01
LON = 1440
OWN = 360
LEFT = 8
J = 384
C = 128
MEM = 4
SLOTS = 4
DEPTH = 3
EXT = SLOTS + 2 * DEPTH
PAD = 8
W = 752
R = 2368
BF = jnp.bfloat16
F32 = jnp.float32
BM = ("band", "member")


def coords(i):
    return [i // 64, i // 16 % 4, i // 4 % 4, i // 2 % 2, i % 2]


def index(v):
    return (((v[0] * 4 + v[1]) * 4 + v[2]) * 2 + v[3]) * 2 + v[4]


SIZES = [2, 4, 4, 2, 2]


def shift(value, dim, by):
    pairs = []
    for i in range(128):
        v = coords(i)
        v[dim] = (v[dim] + by) % SIZES[dim]
        pairs.append((i, index(v)))
    return lax.ppermute(value, BM, pairs)


def scatter_sum(value, dim, place):
    n = SIZES[dim]
    parts = value.reshape(n, value.shape[0] // n, C)
    total = lax.dynamic_index_in_dim(parts, place, 0, keepdims=False)
    got = [
        shift(lax.dynamic_index_in_dim(parts, (place + d) % n, 0, keepdims=False), dim, d)
        for d in range(1, n)
    ]
    for g in got:
        total = total + g
    return total


def exchange_sum(value, dim):
    got = [shift(value, dim, d) for d in range(1, SIZES[dim])]
    for g in got:
        value = value + g
    return value


def gather(value, dim, place):
    n = SIZES[dim]
    got = [shift(value, dim, d) for d in range(1, n)]
    out = jnp.zeros((n,) + value.shape, value.dtype)
    out = lax.dynamic_update_index_in_dim(out, value, place, 0)
    for d, g in enumerate(got, 1):
        out = lax.dynamic_update_index_in_dim(out, g, (place - d) % n, 0)
    return out.reshape(n * value.shape[0], C)


def sigmoid(a):
    return 0.5 * jnp.tanh(0.5 * a) + 0.5


def chip_row(half, src, r, dst, sem):
    cut = LON - (HALF - LEFT)
    left = [
        pltpu.make_async_copy(src.at[r, pl.ds(LON - LEFT, LEFT)], dst.at[pl.ds(0, LEFT)], sem.at[0]),
        pltpu.make_async_copy(
            src.at[r, pl.ds(0, W - LEFT)], dst.at[pl.ds(LEFT, W - LEFT)], sem.at[1]
        ),
    ]
    right = [
        pltpu.make_async_copy(src.at[r, pl.ds(HALF - LEFT, cut)], dst.at[pl.ds(0, cut)], sem.at[0]),
        pltpu.make_async_copy(src.at[r, pl.ds(0, W - cut)], dst.at[pl.ds(cut, W - cut)], sem.at[1]),
    ]
    return [(half == 0, left), (half == 1, right)]


def own_window(quarter, src, dst, sem):
    cut = LON - (3 * OWN - LEFT)
    middle = pl.multiple_of(quarter * OWN - LEFT, 8)
    first = [
        pltpu.make_async_copy(
            src.at[:, pl.ds(LON - LEFT, LEFT)], dst.at[:, pl.ds(0, LEFT)], sem.at[0]
        ),
        pltpu.make_async_copy(
            src.at[:, pl.ds(0, J - LEFT)], dst.at[:, pl.ds(LEFT, J - LEFT)], sem.at[1]
        ),
    ]
    inner = [pltpu.make_async_copy(src.at[:, pl.ds(middle, J)], dst, sem.at[0])]
    last = [
        pltpu.make_async_copy(
            src.at[:, pl.ds(3 * OWN - LEFT, cut)], dst.at[:, pl.ds(0, cut)], sem.at[0]
        ),
        pltpu.make_async_copy(
            src.at[:, pl.ds(0, J - cut)], dst.at[:, pl.ds(cut, J - cut)], sem.at[1]
        ),
    ]
    return [(quarter == 0, first), ((quarter == 1) | (quarter == 2), inner), (quarter == 3, last)]


def start(cases):
    for cond, copies in cases:

        @pl.when(cond)
        def _():
            for c in copies:
                c.start()


def wait(cases):
    for cond, copies in cases:

        @pl.when(cond)
        def _():
            for c in copies:
                c.wait()


def edge_kernel(counts_ref, place_ref, state_ref, target_ref, one_ref, two_ref, three_ref, flag_ref, sem):
    band = place_ref[0]
    member = place_ref[1]
    half, core = member // 2, member % 2
    n = counts_ref[band]
    back = 2 * core - 1
    near = counts_ref[jnp.clip(band + back, 0, 31)]
    far = counts_ref[jnp.clip(band + 2 * back, 0, 31)]
    row = lambda k: jnp.where(core == 0, jnp.maximum(n - 1 - k, 0), k)
    sends = [(state_ref, 0, one_ref, 0), (state_ref, 1, one_ref, 1), (state_ref, 2, one_ref, 2)]
    sends += [(target_ref, 0, one_ref, 3)]
    sends += [(state_ref, 0, two_ref, 0), (state_ref, 1, two_ref, 1), (state_ref, 0, three_ref, 0)]
    cases = []
    for i, (src, k, dst, slot) in enumerate(sends):
        cases += chip_row(half, src, row(k), dst.at[slot], sem.at[i])
    start(cases)
    ones = jnp.ones((1, C), F32)
    flag_ref[0:1] = ones * (near >= 2).astype(F32)
    flag_ref[1:2] = ones * (near >= 3).astype(F32)
    flag_ref[2:3] = ones * (near == 2).astype(F32)
    flag_ref[3:4] = ones * (far >= 2).astype(F32)
    flag_ref[4:8] = jnp.zeros((4, C), F32)
    wait(cases)


def edges(counts, place, state, target):
    smem = pl.BlockSpec(memory_space=pltpu.SMEM)
    vmem = pl.BlockSpec(memory_space=pltpu.VMEM)
    hbm = pl.BlockSpec(memory_space=pl.ANY)
    rows = lambda k: jax.ShapeDtypeStruct((k, W, C), BF)
    return pl.pallas_call(
        edge_kernel,
        out_shape=(rows(4), rows(2), rows(1), jax.ShapeDtypeStruct((8, C), F32)),
        in_specs=[smem, smem, hbm, hbm],
        out_specs=(vmem,) * 4,
        scratch_shapes=[pltpu.SemaphoreType.DMA((7, 2))],
        name="edge_rows",
    )(counts, place, state, target)


def kernel(
    counts_ref, seeds_ref, place_ref, weight_ref,
    state_ref, target_ref, mine_ref, other_ref,
    amp_ref, w1_ref, w2_ref, wt_ref,
    grads_ref, cells_ref,
    state_s, tgt_s, hash_s, buf_s, cbuf_s, crps_s,
    in3_s, hid3_s, cot3_s, pre_s, fc_s, ya_s, yb_s, acc_s, sem,
):
    band = place_ref[0]
    quarter = place_ref[1]
    core = quarter % 2
    n = counts_ref[band]
    offset = lax.fori_loop(0, band, lambda b, s: s + counts_ref[b], jnp.int32(0))

    copies = own_window(quarter, state_ref, state_s.at[pl.ds(DEPTH, SLOTS)], sem.at[0])
    copies += own_window(quarter, target_ref, tgt_s.at[pl.ds(1, SLOTS)], sem.at[1])
    start(copies)

    buf_s[0:PAD] = jnp.zeros((PAD, C), F32)
    buf_s[PAD + J :] = jnp.zeros((PAD, C), F32)

    cols = lax.broadcasted_iota(jnp.int32, (J, C), 0)
    chan = lax.broadcasted_iota(jnp.int32, (J, C), 1)
    lon = quarter * OWN - LEFT + cols
    lon = jnp.where(lon < 0, lon + LON, jnp.where(lon >= LON, lon - LON, lon))
    hash_s[...] = lon * 668265263 + chan * 1274126177
    own_col = ((cols >= LEFT) & (cols < LEFT + OWN)).astype(F32)

    wait(copies)

    def put_edges(above, below):
        for slot, k in ((2, 0), (1, 1), (0, 2)):
            state_s[slot] = above[k]
        for slot, k in ((0, 0), (1, 1), (2, 2)):
            state_s[DEPTH + n + slot] = below[k]
        tgt_s[0] = above[3]
        tgt_s[1 + n] = below[3]

    @pl.when(core == 0)
    def _():
        put_edges(mine_ref, other_ref)

    @pl.when(core == 1)
    def _():
        put_edges(other_ref, mine_ref)

    def valid(e):
        g = offset - DEPTH + e
        return ((g >= 0) & (g < ROWS_TOTAL)).astype(F32)

    def put3(ref, m, e, v):
        buf_s[PAD : PAD + J] = v
        ref[m, e, :, C : 2 * C] = v.astype(BF)
        ref[m, e, :, 0:C] = buf_s[PAD - 1 : PAD - 1 + J].astype(BF)
        ref[m, e, :, 2 * C :] = buf_s[PAD + 1 : PAD + 1 + J].astype(BF)

    amp = amp_ref[...]

    amp_step = amp * (1.0 / 32768.0)
    amp_base = amp * (0.5 / 32768.0 - 1.0)

    def make_inputs(i, _):
        e, m = i // MEM, i % MEM
        g = offset - DEPTH + e
        inside = (g >= 0) & (g < ROWS_TOTAL)

        @pl.when(inside)
        def _():
            h = hash_s[...] + (g * 374761393 + seeds_ref[m] * 1103515245)
            h = h ^ (h >> 13)
            h = h * 1274126177
            h = h ^ (h >> 16)
            v = (state_s[e].astype(F32) + amp_base) + (h & 65535).astype(F32) * amp_step
            put3(in3_s, m, e, v)

        @pl.when(jnp.logical_not(inside))
        def _():
            in3_s[m, e] = jnp.zeros((J, 3 * C), BF)

        return 0

    lax.fori_loop(0, EXT * MEM, make_inputs, 0)

    def conv_pair(ref, m, e, w):
        lhs = jnp.concatenate([ref[m, e + s] for s in range(4)], axis=1)
        return jnp.dot(lhs, w[...], preferred_element_type=F32)

    def make_hidden(i, _):
        p, m = i // MEM, i % MEM
        out = conv_pair(in3_s, m, 2 * p, w1_ref)
        for k in range(2):
            e = 1 + 2 * p + k
            a = out[:, k * C : (k + 1) * C]

            @pl.when((e >= DEPTH) & (e < DEPTH + SLOTS))
            def _():
                pre_s[m, e - DEPTH] = a

            put3(hid3_s, m, e - 1, a * sigmoid(a) * valid(e))
        return 0

    lax.fori_loop(0, 4 * MEM, make_hidden, 0)

    def make_forecast(i, _):
        p, m = i // MEM, i % MEM
        out = conv_pair(hid3_s, m, 2 * p, w2_ref)
        for k in range(2):
            e = 2 + 2 * p + k
            v = (in3_s[m, e, :, C : 2 * C].astype(F32) + out[:, k * C : (k + 1) * C]) * valid(e)
            fc_s[m, e - 2] = v.astype(BF)
        return 0

    lax.fori_loop(0, 3 * MEM, make_forecast, 0)

    pair_scale = 1.0 / (MEM * (MEM - 1))
    factor = 1.0 / math.sqrt(ROWS_TOTAL * LON)

    step = 32

    def make_crps(r, loss):
        e = r + 2
        g = jnp.clip(offset - DEPTH + e, 0, ROWS_TOTAL - 1)
        weight = weight_ref[g] * valid(e)
        mine = ((r >= 1) & (r < 1 + n)).astype(F32)
        scale = weight * (factor * pair_scale)
        slot = jnp.clip(r - 1, 0, SLOTS - 1)

        def chunk(k, _):
            at = pl.ds(pl.multiple_of(k * step, step), step)
            t = tgt_s[r, at].astype(F32)
            f = [fc_s[m, r, at].astype(F32) for m in range(MEM)]
            skill = None
            spread = None
            slopes = []
            for m in range(MEM):
                d = f[m] - t
                q = d * d + SMOOTH
                inv = lax.rsqrt(q)
                skill = q * inv if skill is None else skill + q * inv
                slopes.append(d * inv * (MEM - 1.0))
            for a in range(MEM):
                for b in range(a + 1, MEM):
                    d = f[a] - f[b]
                    q = d * d + SMOOTH
                    inv = lax.rsqrt(q)
                    spread = q * inv if spread is None else spread + q * inv
                    tilt = d * inv
                    slopes[a] = slopes[a] - tilt
                    slopes[b] = slopes[b] + tilt
            crps_s[at] = (skill * (MEM - 1.0) - spread) * pair_scale
            for m in range(MEM):
                cbuf_s[m, pl.ds(pl.multiple_of(PAD + k * step, 8), step)] = slopes[m] * scale
            return 0

        lax.fori_loop(0, J // step, chunk, 0)
        for m in range(MEM):
            mid = cbuf_s[m, PAD : PAD + J]
            cot3_s[m, r, :, C : 2 * C] = mid.astype(BF)
            cot3_s[m, r, :, 0:C] = cbuf_s[m, PAD - 1 : PAD - 1 + J].astype(BF)
            cot3_s[m, r, :, 2 * C :] = cbuf_s[m, PAD + 1 : PAD + 1 + J].astype(BF)

        @pl.when((r >= 1) & (r < 1 + SLOTS))
        def _():
            for m in range(MEM):
                ya_s[m, slot] = (cbuf_s[m, PAD : PAD + J] * (own_col * mine)).astype(BF)
            cells_ref[slot] = jnp.sum(jnp.transpose(crps_s[...]), axis=0, keepdims=True) * (
                weight * mine * (1.0 / C)
            )

        return loss

    for m in range(MEM):
        cbuf_s[m, 0:PAD] = jnp.zeros((PAD, C), F32)
        cbuf_s[m, PAD + J :] = jnp.zeros((PAD, C), F32)
    lax.fori_loop(0, SLOTS + 2, make_crps, 0)
    loss = cells_ref[0] + cells_ref[1] + cells_ref[2] + cells_ref[3]
    lane = lax.broadcasted_iota(jnp.int32, (1, J), 1)
    loss = jnp.where((lane >= LEFT) & (lane < LEFT + OWN), loss, 0.0)

    def make_pre_cot(i, _):
        p, m = i // MEM, i % MEM
        out = conv_pair(cot3_s, m, 2 * p, wt_ref)
        for k in range(2):
            s = 2 * p + k
            a = pre_s[m, s]
            sig = sigmoid(a)
            mine = (s < n).astype(F32)
            v = out[:, k * C : (k + 1) * C] * (sig * (1.0 + a * (1.0 - sig))) * (own_col * mine)
            yb_s[m, s] = v.astype(BF)
        return 0

    lax.fori_loop(0, 2 * MEM, make_pre_cot, 0)

    def weight_grad(x3, first, y, row0):
        acc_s[...] = jnp.zeros_like(acc_s)

        def step(m, _):
            ys = jnp.concatenate(
                [
                    jnp.concatenate([y[m, 0], y[m, 1]], axis=1),
                    jnp.concatenate([y[m, 2], y[m, 3]], axis=1),
                ],
                axis=0,
            )
            for s in range(4):
                xs = jnp.concatenate([x3[m, first + s], x3[m, first + 2 + s]], axis=0)
                acc_s[:, s * 384 : (s + 1) * 384] += lax.dot_general(
                    ys, xs, (((0,), (0,)), ((), ())), preferred_element_type=F32
                )
            return 0

        lax.fori_loop(0, MEM, step, 0)
        for k in range(9):
            blk = acc_s[0:C, k * C : (k + 1) * C] + acc_s[C:, 384 + k * C : 384 + (k + 1) * C]
            grads_ref[row0 + k * C : row0 + (k + 1) * C] = jnp.transpose(blk)

    weight_grad(in3_s, 2, yb_s, 0)
    weight_grad(hid3_s, 1, ya_s, 1152)
    total = jnp.sum(loss, axis=1, keepdims=True) * (1.0 / (ROWS_TOTAL * LON))
    grads_ref[2304:R] = jnp.broadcast_to(total, (R - 2304, C))


def local_step(counts, seeds, place, weights, state, target, mine, other, amp, w1, w2, wt):
    smem = pl.BlockSpec(memory_space=pltpu.SMEM)
    vmem = pl.BlockSpec(memory_space=pltpu.VMEM)
    hbm = pl.BlockSpec(memory_space=pl.ANY)
    return pl.pallas_call(
        kernel,
        out_shape=(
            jax.ShapeDtypeStruct((R, C), F32),
            jax.ShapeDtypeStruct((SLOTS, 1, J), F32),
        ),
        in_specs=[smem] * 4 + [hbm] * 2 + [vmem] * 6,
        out_specs=(vmem, vmem),
        scratch_shapes=[
            pltpu.VMEM((EXT, J, C), BF),
            pltpu.VMEM((SLOTS + 2, J, C), BF),
            pltpu.VMEM((J, C), jnp.int32),
            pltpu.VMEM((J + 2 * PAD, C), F32),
            pltpu.VMEM((MEM, J + 2 * PAD, C), F32),
            pltpu.VMEM((J, C), F32),
            pltpu.VMEM((MEM, EXT, J, 3 * C), BF),
            pltpu.VMEM((MEM, EXT - 2, J, 3 * C), BF),
            pltpu.VMEM((MEM, EXT - 4, J, 3 * C), BF),
            pltpu.VMEM((MEM, SLOTS, J, C), F32),
            pltpu.VMEM((MEM, EXT - 4, J, C), BF),
            pltpu.VMEM((MEM, SLOTS, J, C), BF),
            pltpu.VMEM((MEM, SLOTS, J, C), BF),
            pltpu.VMEM((2 * C, 4 * 384), F32),
            pltpu.SemaphoreType.DMA((2, 2)),
        ],
        compiler_params=pltpu.CompilerParams(vmem_limit_bytes=60 * 1024 * 1024),
        name="ensemble_step",
    )(counts, seeds, place, weights, state, target, mine, other, amp, w1, w2, wt)


def paired(filt):
    flat = filt.reshape(9 * C, C)
    return jnp.concatenate(
        [jnp.pad(flat, ((0, 3 * C), (0, 0))), jnp.pad(flat, ((3 * C, 0), (0, 0)))], axis=1
    )


def body(state, target, amp, filt1, filt2, counts, seed):
    band = lax.axis_index("band")
    member = lax.axis_index("member")
    x = band % 4
    core = member % 2
    weights = jnp.asarray(
        np.cos(np.pi * ((np.arange(ROWS_TOTAL) + 0.5) / GRID_ROWS - 0.5)).astype(np.float32)
    )
    place = jnp.stack([band, member]).astype(jnp.int32)
    seeds = jnp.where(jnp.arange(MEM) == member, seed, 0)
    seeds = seeds + shift(seeds, 4, 1)
    one, two, three, flags = edges(counts, place, state, target)

    def send(value, by):
        pairs = [(i, (i // 4 + by * (1 - 2 * (i % 2))) % 32 * 4 + i % 4) for i in range(128)]
        return lax.ppermute(value, BM, pairs)

    def flag(k):
        return flags[k : k + 1][None] > 0.5

    one, seeds = lax.optimization_barrier((one, seeds))
    g1 = send(one, 1)
    seeds = seeds + shift(seeds, 3, 1)
    two, three, seeds = lax.optimization_barrier((two, three, seeds))
    g2 = send(two, 2)
    g3 = send(three, 3)
    row2 = jnp.where(flag(0), g1[1:2], g2[:1])
    row3 = jnp.where(
        flag(1), g1[2:3], jnp.where(flag(2), g2[:1], jnp.where(flag(3), g2[1:], g3))
    )
    halo = jnp.concatenate([g1[:1], row2, row3, g1[3:]], axis=0)
    mine = lax.dynamic_slice_in_dim(halo, OWN * core, J, 1)
    other = shift(lax.dynamic_slice_in_dim(halo, OWN * (1 - core), J, 1), 4, 1)

    w1 = paired(filt1)
    w2 = paired(filt2)
    wt = paired(jnp.transpose(filt2[::-1, ::-1], (0, 1, 3, 2)))
    grads, cells = local_step(
        counts, seeds, place, weights, state, target, mine, other, amp[None], w1, w2, wt
    )

    part = scatter_sum(grads, 4, core)
    part = scatter_sum(part, 2, x)
    part = exchange_sum(part, 1)
    part = exchange_sum(part, 3)
    part = exchange_sum(part, 0)
    part = gather(part, 2, x)
    full = gather(part, 4, core)

    return (
        cells[:, 0, LEFT : LEFT + OWN],
        full[2304, 0],
        full[:1152].reshape(3, 3, C, C),
        full[1152:2304].reshape(3, 3, C, C),
    )


def solution(mesh):
    in_specs = (P("band", None, None), P("band", None, None), P(), P(), P(), P(), P("member"))
    out_specs = (P("band", "member"), P(), P(), P())
    return jax.shard_map(body, mesh=mesh, in_specs=in_specs, out_specs=out_specs, check_vma=False)
```

```python
import math

import jax
import jax.numpy as jnp
import numpy as np
from jax import lax
from jax.experimental import pallas as pl
from jax.experimental.pallas import tpu as pltpu
from jax.sharding import PartitionSpec as P

GRID_ROWS = 721
HALF = 720
ROWS_TOTAL = 96
SMOOTH = 0.01
LON = 1440
OWN = 360
LEFT = 8
J = 384
C = 128
MEM = 4
SLOTS = 4
DEPTH = 3
EXT = SLOTS + 2 * DEPTH
PAD = 8
W = 752
R = 2368
BF = jnp.bfloat16
F32 = jnp.float32
BM = ("band", "member")


def coords(i):
    return [i // 64, i // 16 % 4, i // 4 % 4, i // 2 % 2, i % 2]


def index(v):
    return (((v[0] * 4 + v[1]) * 4 + v[2]) * 2 + v[3]) * 2 + v[4]


SIZES = [2, 4, 4, 2, 2]


def shift(value, dim, by):
    pairs = []
    for i in range(128):
        v = coords(i)
        v[dim] = (v[dim] + by) % SIZES[dim]
        pairs.append((i, index(v)))
    return lax.ppermute(value, BM, pairs)


def scatter_sum(value, dim, place):
    n = SIZES[dim]
    parts = value.reshape(n, value.shape[0] // n, C)
    total = lax.dynamic_index_in_dim(parts, place, 0, keepdims=False)
    got = [
        shift(lax.dynamic_index_in_dim(parts, (place + d) % n, 0, keepdims=False), dim, d)
        for d in range(1, n)
    ]
    for g in got:
        total = total + g
    return total


def exchange_sum(value, dim):
    got = [shift(value, dim, d) for d in range(1, SIZES[dim])]
    for g in got:
        value = value + g
    return value


def gather(value, dim, place):
    n = SIZES[dim]
    got = [shift(value, dim, d) for d in range(1, n)]
    out = jnp.zeros((n,) + value.shape, value.dtype)
    out = lax.dynamic_update_index_in_dim(out, value, place, 0)
    for d, g in enumerate(got, 1):
        out = lax.dynamic_update_index_in_dim(out, g, (place - d) % n, 0)
    return out.reshape(n * value.shape[0], C)


def chip_row(half, src, r, dst, sem):
    cut = LON - (HALF - LEFT)
    left = [
        pltpu.make_async_copy(src.at[r, pl.ds(LON - LEFT, LEFT)], dst.at[pl.ds(0, LEFT)], sem.at[0]),
        pltpu.make_async_copy(
            src.at[r, pl.ds(0, W - LEFT)], dst.at[pl.ds(LEFT, W - LEFT)], sem.at[1]
        ),
    ]
    right = [
        pltpu.make_async_copy(src.at[r, pl.ds(HALF - LEFT, cut)], dst.at[pl.ds(0, cut)], sem.at[0]),
        pltpu.make_async_copy(src.at[r, pl.ds(0, W - cut)], dst.at[pl.ds(cut, W - cut)], sem.at[1]),
    ]
    return [(half == 0, left), (half == 1, right)]


def own_window(quarter, src, dst, sem):
    cut = LON - (3 * OWN - LEFT)
    middle = pl.multiple_of(quarter * OWN - LEFT, 8)
    first = [
        pltpu.make_async_copy(
            src.at[:, pl.ds(LON - LEFT, LEFT)], dst.at[:, pl.ds(0, LEFT)], sem.at[0]
        ),
        pltpu.make_async_copy(
            src.at[:, pl.ds(0, J - LEFT)], dst.at[:, pl.ds(LEFT, J - LEFT)], sem.at[1]
        ),
    ]
    inner = [pltpu.make_async_copy(src.at[:, pl.ds(middle, J)], dst, sem.at[0])]
    last = [
        pltpu.make_async_copy(
            src.at[:, pl.ds(3 * OWN - LEFT, cut)], dst.at[:, pl.ds(0, cut)], sem.at[0]
        ),
        pltpu.make_async_copy(
            src.at[:, pl.ds(0, J - cut)], dst.at[:, pl.ds(cut, J - cut)], sem.at[1]
        ),
    ]
    return [(quarter == 0, first), ((quarter == 1) | (quarter == 2), inner), (quarter == 3, last)]


def start(cases):
    for cond, copies in cases:

        @pl.when(cond)
        def _():
            for c in copies:
                c.start()


def wait(cases):
    for cond, copies in cases:

        @pl.when(cond)
        def _():
            for c in copies:
                c.wait()


def edge_kernel(counts_ref, place_ref, state_ref, target_ref, one_ref, two_ref, three_ref, flag_ref, sem):
    band = place_ref[0]
    member = place_ref[1]
    half, core = member // 2, member % 2
    n = counts_ref[band]
    back = 2 * core - 1
    near = counts_ref[jnp.clip(band + back, 0, 31)]
    far = counts_ref[jnp.clip(band + 2 * back, 0, 31)]
    row = lambda k: jnp.where(core == 0, jnp.maximum(n - 1 - k, 0), k)
    sends = [(state_ref, 0, one_ref, 0), (state_ref, 1, one_ref, 1), (state_ref, 2, one_ref, 2)]
    sends += [(target_ref, 0, one_ref, 3)]
    sends += [(state_ref, 0, two_ref, 0), (state_ref, 1, two_ref, 1), (state_ref, 0, three_ref, 0)]
    cases = []
    for i, (src, k, dst, slot) in enumerate(sends):
        cases += chip_row(half, src, row(k), dst.at[slot], sem.at[i])
    start(cases)
    ones = jnp.ones((1, C), F32)
    flag_ref[0:1] = ones * (near >= 2).astype(F32)
    flag_ref[1:2] = ones * (near >= 3).astype(F32)
    flag_ref[2:3] = ones * (near == 2).astype(F32)
    flag_ref[3:4] = ones * (far >= 2).astype(F32)
    flag_ref[4:8] = jnp.zeros((4, C), F32)
    wait(cases)


def edges(counts, place, state, target):
    smem = pl.BlockSpec(memory_space=pltpu.SMEM)
    vmem = pl.BlockSpec(memory_space=pltpu.VMEM)
    hbm = pl.BlockSpec(memory_space=pl.ANY)
    rows = lambda k: jax.ShapeDtypeStruct((k, W, C), BF)
    return pl.pallas_call(
        edge_kernel,
        out_shape=(rows(4), rows(2), rows(1), jax.ShapeDtypeStruct((8, C), F32)),
        in_specs=[smem, smem, hbm, hbm],
        out_specs=(vmem,) * 4,
        scratch_shapes=[pltpu.SemaphoreType.DMA((7, 2))],
        name="edge_rows",
    )(counts, place, state, target)


def kernel(
    counts_ref, seeds_ref, place_ref, weight_ref,
    state_ref, target_ref, mine_ref, other_ref,
    amp_ref, w1_ref, w2_ref, wt_ref,
    grads_ref, cells_ref,
    state_s, tgt_s, hash_s, bufs, cbuf_s, crps_s,
    in3, hid3, cot3_s, pre_s, fc_s, ya_s, yb_s, acc_s, sem,
):
    band = place_ref[0]
    quarter = place_ref[1]
    core = quarter % 2
    n = counts_ref[band]
    offset = lax.fori_loop(0, band, lambda b, s: s + counts_ref[b], jnp.int32(0))

    copies = own_window(quarter, state_ref, state_s.at[pl.ds(DEPTH, SLOTS)], sem.at[0])
    copies += own_window(quarter, target_ref, tgt_s.at[pl.ds(1, SLOTS)], sem.at[1])
    start(copies)

    for buf in bufs:
        buf[0:PAD] = jnp.zeros((PAD, C), F32)
        buf[PAD + J :] = jnp.zeros((PAD, C), F32)

    cols = lax.broadcasted_iota(jnp.int32, (J, C), 0)
    chan = lax.broadcasted_iota(jnp.int32, (J, C), 1)
    lon = quarter * OWN - LEFT + cols
    lon = jnp.where(lon < 0, lon + LON, jnp.where(lon >= LON, lon - LON, lon))
    hash_s[...] = lon * 668265263 + chan * 1274126177

    wait(copies)

    def put_edges(above, below):
        for slot, k in ((2, 0), (1, 1), (0, 2)):
            state_s[slot] = above[k]
        for slot, k in ((0, 0), (1, 1), (2, 2)):
            state_s[DEPTH + n + slot] = below[k]
        tgt_s[0] = above[3]
        tgt_s[1 + n] = below[3]

    @pl.when(core == 0)
    def _():
        put_edges(mine_ref, other_ref)

    @pl.when(core == 1)
    def _():
        put_edges(other_ref, mine_ref)

    def outside(e):
        g = offset - DEPTH + e
        return (g < 0) | (g >= ROWS_TOTAL)

    def trim(ref, m, slot):
        ref[m, slot, 0:LEFT] = jnp.zeros((LEFT, C), BF)
        ref[m, slot, LEFT + OWN :] = jnp.zeros((J - OWN - LEFT, C), BF)

    for e in (0, 1, 2):

        @pl.when(outside(e))
        def _():
            state_s[e] = jnp.zeros((J, C), BF)

    for e in range(DEPTH + 1, EXT):

        @pl.when(outside(e))
        def _():
            state_s[e] = jnp.zeros((J, C), BF)

    turn = [0]

    def put3(ref, m, slot, v):
        buf = bufs[turn[0] % len(bufs)]
        turn[0] += 1
        buf[PAD : PAD + J] = v
        ref[m, slot, :, C : 2 * C] = v.astype(BF)
        ref[m, slot, :, 0:C] = buf[PAD - 1 : PAD - 1 + J].astype(BF)
        ref[m, slot, :, 2 * C :] = buf[PAD + 1 : PAD + 1 + J].astype(BF)

    amp = amp_ref[...]
    amp_step = amp * (1.0 / 32768.0)
    amp_base = amp * (0.5 / 32768.0 - 1.0)

    def make_inputs(m, k):
        seed = seeds_ref[jnp.minimum(m, MEM - 1)] * 1103515245
        for j in range(2):
            e = 2 * k + j
            live = jnp.where(outside(e), 0.0, 1.0)
            h = hash_s[...] + ((offset - DEPTH + e) * 374761393 + seed)
            h = h ^ (h >> 13)
            h = h * 1274126177
            h = h ^ (h >> 16)
            v = (state_s[e].astype(F32) + amp_base * live) + (h & 65535).astype(F32) * (
                amp_step * live
            )
            put3(in3[k], m, j, v)

    def conv_pair(top, bottom, m, w):
        lhs = jnp.concatenate([top[m, 0], top[m, 1], bottom[m, 0], bottom[m, 1]], axis=1)
        return jnp.dot(lhs, w[...], preferred_element_type=F32)

    def make_hidden(m, p):
        out = conv_pair(in3[p], in3[p + 1], m, w1_ref)
        for j in range(2):
            e = 1 + 2 * p + j
            a = out[:, j * C : (j + 1) * C]
            if DEPTH <= e < DEPTH + SLOTS:
                pre_s[m, e - DEPTH] = a
            half = jnp.where(outside(e), 0.0, 0.5)
            put3(hid3[p], m, j, (a * half) * (1.0 + jnp.tanh(0.5 * a)))

    def make_forecast(m, p):
        out = conv_pair(hid3[p], hid3[p + 1], m, w2_ref)
        for j in range(2):
            v = in3[p + 1][m, j, :, C : 2 * C].astype(F32) + out[:, j * C : (j + 1) * C]
            fc_s[m, 2 * p + j] = v.astype(BF)

    def member(m, _):
        make_inputs(m, 0)
        make_inputs(m, 1)
        make_inputs(m, 2)
        make_hidden(m, 0)
        make_inputs(m, 3)
        make_hidden(m, 1)
        make_inputs(m, 4)
        make_forecast(m, 0)
        make_hidden(m, 2)
        make_forecast(m, 1)
        make_hidden(m, 3)
        make_forecast(m, 2)
        return 0

    lax.fori_loop(0, MEM, member, 0)

    pair_scale = 1.0 / (MEM * (MEM - 1))
    factor = 1.0 / math.sqrt(ROWS_TOTAL * LON)

    step = 32

    def make_crps(r, loss):
        e = r + 2
        g = jnp.clip(offset - DEPTH + e, 0, ROWS_TOTAL - 1)
        weight = jnp.where(outside(e), 0.0, weight_ref[g])
        mine = ((r >= 1) & (r < 1 + n)).astype(F32)
        scale = weight * (factor * pair_scale)
        slot = jnp.clip(r - 1, 0, SLOTS - 1)

        def chunk(k, _):
            at = pl.ds(pl.multiple_of(k * step, step), step)
            t = tgt_s[r, at].astype(F32)
            f = [fc_s[m, r, at].astype(F32) for m in range(MEM)]
            skill = None
            spread = None
            slopes = []
            for m in range(MEM):
                d = f[m] - t
                q = d * d + SMOOTH
                inv = lax.rsqrt(q)
                skill = q * inv if skill is None else skill + q * inv
                slopes.append(d * inv * (MEM - 1.0))
            for a in range(MEM):
                for b in range(a + 1, MEM):
                    d = f[a] - f[b]
                    q = d * d + SMOOTH
                    inv = lax.rsqrt(q)
                    spread = q * inv if spread is None else spread + q * inv
                    tilt = d * inv
                    slopes[a] = slopes[a] - tilt
                    slopes[b] = slopes[b] + tilt
            crps_s[at] = (skill * (MEM - 1.0) - spread) * pair_scale
            for m in range(MEM):
                cbuf_s[m, pl.ds(pl.multiple_of(PAD + k * step, 8), step)] = slopes[m] * scale
            return 0

        lax.fori_loop(0, J // step, chunk, 0)
        for m in range(MEM):
            mid = cbuf_s[m, PAD : PAD + J]
            cot3_s[m, r, :, C : 2 * C] = mid.astype(BF)
            cot3_s[m, r, :, 0:C] = cbuf_s[m, PAD - 1 : PAD - 1 + J].astype(BF)
            cot3_s[m, r, :, 2 * C :] = cbuf_s[m, PAD + 1 : PAD + 1 + J].astype(BF)

        @pl.when((r >= 1) & (r < 1 + SLOTS))
        def _():
            for m in range(MEM):
                ya_s[m, slot] = cot3_s[m, r, :, C : 2 * C]
                trim(ya_s, m, slot)
            @pl.when(r > n)
            def _():
                ya_s[:, slot] = jnp.zeros((MEM, J, C), BF)

            cells_ref[slot] = jnp.sum(jnp.transpose(crps_s[...]), axis=0, keepdims=True) * (
                weight * mine * (1.0 / C)
            )

        return loss

    for m in range(MEM):
        cbuf_s[m, 0:PAD] = jnp.zeros((PAD, C), F32)
        cbuf_s[m, PAD + J :] = jnp.zeros((PAD, C), F32)
    lax.fori_loop(0, SLOTS + 2, make_crps, 0)
    loss = cells_ref[0] + cells_ref[1] + cells_ref[2] + cells_ref[3]
    lane = lax.broadcasted_iota(jnp.int32, (1, J), 1)
    loss = jnp.where((lane >= LEFT) & (lane < LEFT + OWN), loss, 0.0)

    def make_pre_cot(i, _):
        p, m = i // MEM, i % MEM
        lhs = jnp.concatenate([cot3_s[m, 2 * p + r] for r in range(4)], axis=1)
        out = jnp.dot(lhs, wt_ref[...], preferred_element_type=F32)
        for k in range(2):
            s = 2 * p + k
            a = pre_s[m, s]
            t = jnp.tanh(0.5 * a)
            mine = jnp.where(s < n, 0.25, 0.0)
            v = out[:, k * C : (k + 1) * C] * (((1.0 + t) * mine) * (2.0 + a * (1.0 - t)))
            yb_s[m, s] = v.astype(BF)
            trim(yb_s, m, s)
        return 0

    lax.fori_loop(0, 2 * MEM, make_pre_cot, 0)

    def weight_grad(rows, y, row0):
        acc_s[...] = jnp.zeros_like(acc_s)

        def step(m, _):
            ys = jnp.concatenate(
                [
                    jnp.concatenate([y[m, 0], y[m, 1]], axis=1),
                    jnp.concatenate([y[m, 2], y[m, 3]], axis=1),
                ],
                axis=0,
            )
            xs = jnp.concatenate(
                [
                    jnp.concatenate([ref[m, j] for ref, j in rows[a : a + 4]], axis=1)
                    for a in (0, 2)
                ],
                axis=0,
            )
            acc_s[...] += lax.dot_general(
                ys, xs, (((0,), (0,)), ((), ())), preferred_element_type=F32
            )
            return 0

        lax.fori_loop(0, MEM, step, 0)
        for k in range(9):
            blk = acc_s[0:C, k * C : (k + 1) * C] + acc_s[C:, 384 + k * C : 384 + (k + 1) * C]
            grads_ref[row0 + k * C : row0 + (k + 1) * C] = jnp.transpose(blk)

    weight_grad([(in3[e // 2], e % 2) for e in range(2, 8)], yb_s, 0)
    weight_grad([(hid3[(e - 1) // 2], (e - 1) % 2) for e in range(2, 8)], ya_s, 1152)
    total = jnp.sum(loss, axis=1, keepdims=True) * (1.0 / (ROWS_TOTAL * LON))
    grads_ref[2304:R] = jnp.broadcast_to(total, (R - 2304, C))


def local_step(counts, seeds, place, weights, state, target, mine, other, amp, w1, w2, wt):
    smem = pl.BlockSpec(memory_space=pltpu.SMEM)
    vmem = pl.BlockSpec(memory_space=pltpu.VMEM)
    hbm = pl.BlockSpec(memory_space=pl.ANY)
    return pl.pallas_call(
        kernel,
        out_shape=(
            jax.ShapeDtypeStruct((R, C), F32),
            jax.ShapeDtypeStruct((SLOTS, 1, J), F32),
        ),
        in_specs=[smem] * 4 + [hbm] * 2 + [vmem] * 6,
        out_specs=(vmem, vmem),
        scratch_shapes=[
            pltpu.VMEM((EXT, J, C), BF),
            pltpu.VMEM((SLOTS + 2, J, C), BF),
            pltpu.VMEM((J, C), jnp.int32),
            [pltpu.VMEM((J + 2 * PAD, C), F32) for _ in range(6)],
            pltpu.VMEM((MEM, J + 2 * PAD, C), F32),
            pltpu.VMEM((J, C), F32),
            [pltpu.VMEM((MEM + (k < 3), 2, J, 3 * C), BF) for k in range(5)],
            [pltpu.VMEM((MEM, 2, J, 3 * C), BF) for _ in range(4)],
            pltpu.VMEM((MEM, EXT - 4, J, 3 * C), BF),
            pltpu.VMEM((MEM, SLOTS, J, C), F32),
            pltpu.VMEM((MEM, EXT - 4, J, C), BF),
            pltpu.VMEM((MEM, SLOTS, J, C), BF),
            pltpu.VMEM((MEM, SLOTS, J, C), BF),
            pltpu.VMEM((2 * C, 4 * 384), F32),
            pltpu.SemaphoreType.DMA((2, 2)),
        ],
        compiler_params=pltpu.CompilerParams(vmem_limit_bytes=60 * 1024 * 1024),
        name="ensemble_step",
    )(counts, seeds, place, weights, state, target, mine, other, amp, w1, w2, wt)


def paired(filt):
    flat = filt.reshape(9 * C, C)
    return jnp.concatenate(
        [jnp.pad(flat, ((0, 3 * C), (0, 0))), jnp.pad(flat, ((3 * C, 0), (0, 0)))], axis=1
    )


def body(state, target, amp, filt1, filt2, counts, seed):
    band = lax.axis_index("band")
    member = lax.axis_index("member")
    x = band % 4
    core = member % 2
    weights = jnp.asarray(
        np.cos(np.pi * ((np.arange(ROWS_TOTAL) + 0.5) / GRID_ROWS - 0.5)).astype(np.float32)
    )
    place = jnp.stack([band, member]).astype(jnp.int32)
    seeds = jnp.where(jnp.arange(MEM) == member, seed, 0)
    seeds = seeds + shift(seeds, 4, 1)
    one, two, three, flags = edges(counts, place, state, target)

    def send(value, by):
        pairs = [(i, (i // 4 + by * (1 - 2 * (i % 2))) % 32 * 4 + i % 4) for i in range(128)]
        return lax.ppermute(value, BM, pairs)

    def flag(k):
        return flags[k : k + 1][None] > 0.5

    one, seeds = lax.optimization_barrier((one, seeds))
    g1 = send(one, 1)
    seeds = seeds + shift(seeds, 3, 1)
    two, three, seeds = lax.optimization_barrier((two, three, seeds))
    g2 = send(two, 2)
    g3 = send(three, 3)
    row2 = jnp.where(flag(0), g1[1:2], g2[:1])
    row3 = jnp.where(
        flag(1), g1[2:3], jnp.where(flag(2), g2[:1], jnp.where(flag(3), g2[1:], g3))
    )
    halo = jnp.concatenate([g1[:1], row2, row3, g1[3:]], axis=0)
    mine = lax.dynamic_slice_in_dim(halo, OWN * core, J, 1)
    other = shift(lax.dynamic_slice_in_dim(halo, OWN * (1 - core), J, 1), 4, 1)

    w1 = paired(filt1)
    w2 = paired(filt2)
    wt = paired(jnp.transpose(filt2[::-1, ::-1], (0, 1, 3, 2)))
    grads, cells = local_step(
        counts, seeds, place, weights, state, target, mine, other, amp[None], w1, w2, wt
    )

    part = scatter_sum(grads, 4, core)
    part = scatter_sum(part, 2, x)
    part = exchange_sum(part, 1)
    part = exchange_sum(part, 3)
    part = exchange_sum(part, 0)
    part = gather(part, 2, x)
    full = gather(part, 4, core)

    return (
        cells[:, 0, LEFT : LEFT + OWN],
        full[2304, 0],
        full[:1152].reshape(3, 3, C, C),
        full[1152:2304].reshape(3, 3, C, C),
    )


def solution(mesh):
    in_specs = (P("band", None, None), P("band", None, None), P(), P(), P(), P(), P("member"))
    out_specs = (P("band", "member"), P(), P(), P())
    return jax.shard_map(body, mesh=mesh, in_specs=in_specs, out_specs=out_specs, check_vma=False)
```

```python
import math

import jax
import jax.numpy as jnp
import numpy as np
from jax import lax
from jax.experimental import pallas as pl
from jax.experimental.pallas import tpu as pltpu
from jax.sharding import PartitionSpec as P

GRID_ROWS = 721
HALF = 720
ROWS_TOTAL = 96
SMOOTH = 0.01
LON = 1440
OWN = 360
LEFT = 8
J = 384
C = 128
MEM = 4
SLOTS = 4
DEPTH = 3
EXT = SLOTS + 2 * DEPTH
PAD = 8
W = 752
G = 1152
TAIL = 16
BF = jnp.bfloat16
F32 = jnp.float32
BM = ("band", "member")


def coords(i):
    return [i // 64, i // 16 % 4, i // 4 % 4, i // 2 % 2, i % 2]


def index(v):
    return (((v[0] * 4 + v[1]) * 4 + v[2]) * 2 + v[3]) * 2 + v[4]


SIZES = [2, 4, 4, 2, 2]


def permute(value, move):
    return lax.ppermute(value, BM, [(i, index(move(coords(i)))) for i in range(128)])


def shift(value, dim, by):
    def move(v):
        v[dim] = (v[dim] + by) % SIZES[dim]
        return v

    return permute(value, move)


def shift_z(value, by):
    def move(v):
        z = (2 * v[3] + v[0] + by) % 4
        v[3], v[0] = z // 2, z % 2
        return v

    return permute(value, move)


def root(bound):
    return half(jnp.sqrt(jnp.maximum(bound, 2.0**-24)) * 1.001)


def half(value):
    return lax.reduce_precision(value, exponent_bits=5, mantissa_bits=10)


def encode(value, bound, loss):
    r = root(bound)
    q = (value * (1.0 / (r * r))).astype(jnp.float16)
    rl = root(jnp.abs(loss))
    share = loss * (1.0 / (rl * rl))
    high = half(share)
    low = (share - high) * 1024.0
    tail = jnp.concatenate([r, rl, high, low, jnp.zeros((TAIL - 4, C), F32)], axis=0)
    return q, tail.astype(jnp.float16)


def decode(message):
    q, tail = message[:-TAIL].astype(F32), message[-TAIL:].astype(F32)
    r, rl = tail[0:1], tail[1:2]
    scale = r * r
    return q * scale, scale, (tail[2:3] + tail[3:4] * (1.0 / 1024.0)) * (rl * rl)


def ordered(own, got, place):
    out = jnp.zeros((len(got) + 1,) + own.shape, own.dtype)
    out = lax.dynamic_update_index_in_dim(out, own, place, 0)
    for d, g in enumerate(got, 1):
        out = lax.dynamic_update_index_in_dim(out, g, (place - d) % (len(got) + 1), 0)
    return out


def total(messages):
    parts = [decode(messages[k]) for k in range(messages.shape[0])]
    value, bound, loss = parts[0]
    for v, b, l in parts[1:]:
        value, bound, loss = value + v, bound + b, loss + l
    return value, bound, loss


def reduce_all(kept, sent, band, member):
    core = member % 2
    x, y = band % 4, band // 4 % 4
    z = 2 * (member // 2) + band // 16
    got = shift(sent, 4, 1)
    value = kept[:G] + got[:G]
    bound = kept[G : G + 1] + got[G : G + 1]
    loss = kept[G + 1 : G + 2] + got[G + 1 : G + 2]

    q, tail = encode(value, bound, loss)
    parts = q.reshape(4, G // 4, C)

    def part(k):
        return jnp.concatenate([lax.dynamic_index_in_dim(parts, k, 0, keepdims=False), tail], axis=0)

    got = [shift(part((x + d) % 4), 2, d) for d in range(1, 4)]
    value, bound, loss = total(ordered(part(x), got, x))

    message = jnp.concatenate(encode(value, bound, loss), axis=0)
    value, bound, loss = total(ordered(message, [shift(message, 1, d) for d in range(1, 4)], y))

    message = jnp.concatenate(encode(value, bound, loss), axis=0)
    value, bound, loss = total(ordered(message, [shift_z(message, d) for d in range(1, 4)], z))

    message = jnp.concatenate(encode(value, bound, loss), axis=0)
    messages = ordered(message, [shift(message, 2, d) for d in range(1, 4)], x)
    value = jnp.concatenate([decode(messages[k])[0] for k in range(4)], axis=0)
    other = shift(value, 4, 1)
    first = jnp.where(core == 0, value, other)
    second = jnp.where(core == 0, other, value)
    return loss[0, 0], first.reshape(3, 3, C, C), second.reshape(3, 3, C, C)


def chip_row(half, src, r, dst, sem):
    cut = LON - (HALF - LEFT)
    left = [
        pltpu.make_async_copy(src.at[r, pl.ds(LON - LEFT, LEFT)], dst.at[pl.ds(0, LEFT)], sem.at[0]),
        pltpu.make_async_copy(
            src.at[r, pl.ds(0, W - LEFT)], dst.at[pl.ds(LEFT, W - LEFT)], sem.at[1]
        ),
    ]
    right = [
        pltpu.make_async_copy(src.at[r, pl.ds(HALF - LEFT, cut)], dst.at[pl.ds(0, cut)], sem.at[0]),
        pltpu.make_async_copy(src.at[r, pl.ds(0, W - cut)], dst.at[pl.ds(cut, W - cut)], sem.at[1]),
    ]
    return [(half == 0, left), (half == 1, right)]


def own_window(quarter, src, dst, sem):
    cut = LON - (3 * OWN - LEFT)
    middle = pl.multiple_of(quarter * OWN - LEFT, 8)
    first = [
        pltpu.make_async_copy(
            src.at[:, pl.ds(LON - LEFT, LEFT)], dst.at[:, pl.ds(0, LEFT)], sem.at[0]
        ),
        pltpu.make_async_copy(
            src.at[:, pl.ds(0, J - LEFT)], dst.at[:, pl.ds(LEFT, J - LEFT)], sem.at[1]
        ),
    ]
    inner = [pltpu.make_async_copy(src.at[:, pl.ds(middle, J)], dst, sem.at[0])]
    last = [
        pltpu.make_async_copy(
            src.at[:, pl.ds(3 * OWN - LEFT, cut)], dst.at[:, pl.ds(0, cut)], sem.at[0]
        ),
        pltpu.make_async_copy(
            src.at[:, pl.ds(0, J - cut)], dst.at[:, pl.ds(cut, J - cut)], sem.at[1]
        ),
    ]
    return [(quarter == 0, first), ((quarter == 1) | (quarter == 2), inner), (quarter == 3, last)]


def start(cases):
    for cond, copies in cases:

        @pl.when(cond)
        def _():
            for c in copies:
                c.start()


def wait(cases):
    for cond, copies in cases:

        @pl.when(cond)
        def _():
            for c in copies:
                c.wait()


def edge_kernel(counts_ref, place_ref, state_ref, target_ref, one_ref, two_ref, three_ref, flag_ref, sem):
    band = place_ref[0]
    member = place_ref[1]
    half, core = member // 2, member % 2
    n = counts_ref[band]
    back = 2 * core - 1
    near = counts_ref[jnp.clip(band + back, 0, 31)]
    far = counts_ref[jnp.clip(band + 2 * back, 0, 31)]
    row = lambda k: jnp.where(core == 0, jnp.maximum(n - 1 - k, 0), k)
    sends = [(state_ref, 0, one_ref, 0), (state_ref, 1, one_ref, 1), (state_ref, 2, one_ref, 2)]
    sends += [(target_ref, 0, one_ref, 3)]
    sends += [(state_ref, 0, two_ref, 0), (state_ref, 1, two_ref, 1), (state_ref, 0, three_ref, 0)]
    cases = []
    for i, (src, k, dst, slot) in enumerate(sends):
        cases += chip_row(half, src, row(k), dst.at[slot], sem.at[i])
    start(cases)
    ones = jnp.ones((1, C), F32)
    flag_ref[0:1] = ones * (near >= 2).astype(F32)
    flag_ref[1:2] = ones * (near >= 3).astype(F32)
    flag_ref[2:3] = ones * (near == 2).astype(F32)
    flag_ref[3:4] = ones * (far >= 2).astype(F32)
    flag_ref[4:8] = jnp.zeros((4, C), F32)
    wait(cases)


def edges(counts, place, state, target):
    smem = pl.BlockSpec(memory_space=pltpu.SMEM)
    vmem = pl.BlockSpec(memory_space=pltpu.VMEM)
    hbm = pl.BlockSpec(memory_space=pl.ANY)
    rows = lambda k: jax.ShapeDtypeStruct((k, W, C), BF)
    return pl.pallas_call(
        edge_kernel,
        out_shape=(rows(4), rows(2), rows(1), jax.ShapeDtypeStruct((8, C), F32)),
        in_specs=[smem, smem, hbm, hbm],
        out_specs=(vmem,) * 4,
        scratch_shapes=[pltpu.SemaphoreType.DMA((7, 2))],
        name="edge_rows",
    )(counts, place, state, target)


def kernel(
    counts_ref, seeds_ref, place_ref, weight_ref,
    state_ref, target_ref, mine_ref, other_ref,
    amp_ref, w1_ref, w2_ref, wt_ref,
    grads_ref, cells_ref,
    state_s, tgt_s, hash_s, bufs, cbuf_s, crps_s,
    in3, hid3, cot3_s, pre_s, fc_s, ya_s, yb_s, acc_s, sem,
):
    band = place_ref[0]
    quarter = place_ref[1]
    core = quarter % 2
    n = counts_ref[band]
    offset = lax.fori_loop(0, band, lambda b, s: s + counts_ref[b], jnp.int32(0))

    copies = own_window(quarter, state_ref, state_s.at[pl.ds(DEPTH, SLOTS)], sem.at[0])
    copies += own_window(quarter, target_ref, tgt_s.at[pl.ds(1, SLOTS)], sem.at[1])
    start(copies)

    for buf in bufs:
        buf[0:PAD] = jnp.zeros((PAD, C), F32)
        buf[PAD + J :] = jnp.zeros((PAD, C), F32)

    cols = lax.broadcasted_iota(jnp.int32, (J, C), 0)
    chan = lax.broadcasted_iota(jnp.int32, (J, C), 1)
    lon = quarter * OWN - LEFT + cols
    lon = jnp.where(lon < 0, lon + LON, jnp.where(lon >= LON, lon - LON, lon))
    hash_s[...] = lon * 668265263 + chan * 1274126177

    wait(copies)

    def put_edges(above, below):
        for slot, k in ((2, 0), (1, 1), (0, 2)):
            state_s[slot] = above[k]
        for slot, k in ((0, 0), (1, 1), (2, 2)):
            state_s[DEPTH + n + slot] = below[k]
        tgt_s[0] = above[3]
        tgt_s[1 + n] = below[3]

    @pl.when(core == 0)
    def _():
        put_edges(mine_ref, other_ref)

    @pl.when(core == 1)
    def _():
        put_edges(other_ref, mine_ref)

    def outside(e):
        g = offset - DEPTH + e
        return (g < 0) | (g >= ROWS_TOTAL)

    def trim(ref, m, slot):
        ref[m, slot, 0:LEFT] = jnp.zeros((LEFT, C), BF)
        ref[m, slot, LEFT + OWN :] = jnp.zeros((J - OWN - LEFT, C), BF)

    for e in (0, 1, 2):

        @pl.when(outside(e))
        def _():
            state_s[e] = jnp.zeros((J, C), BF)

    for e in range(DEPTH + 1, EXT):

        @pl.when(outside(e))
        def _():
            state_s[e] = jnp.zeros((J, C), BF)

    turn = [0]

    def put3(ref, m, slot, v):
        buf = bufs[turn[0] % len(bufs)]
        turn[0] += 1
        buf[PAD : PAD + J] = v
        ref[m, slot, :, C : 2 * C] = v.astype(BF)
        ref[m, slot, :, 0:C] = buf[PAD - 1 : PAD - 1 + J].astype(BF)
        ref[m, slot, :, 2 * C :] = buf[PAD + 1 : PAD + 1 + J].astype(BF)

    amp = amp_ref[...]
    amp_step = amp * (1.0 / 32768.0)
    amp_base = amp * (0.5 / 32768.0 - 1.0)

    def make_inputs(m, k):
        seed = seeds_ref[jnp.minimum(m, MEM - 1)] * 1103515245
        for j in range(2):
            e = 2 * k + j
            live = jnp.where(outside(e), 0.0, 1.0)
            h = hash_s[...] + ((offset - DEPTH + e) * 374761393 + seed)
            h = h ^ (h >> 13)
            h = h * 1274126177
            h = h ^ (h >> 16)
            v = (state_s[e].astype(F32) + amp_base * live) + (h & 65535).astype(F32) * (
                amp_step * live
            )
            put3(in3[k], m, j, v)

    def conv_pair(top, bottom, m, w):
        lhs = jnp.concatenate([top[m, 0], top[m, 1], bottom[m, 0], bottom[m, 1]], axis=1)
        return jnp.dot(lhs, w[...], preferred_element_type=F32)

    def make_hidden(m, p):
        out = conv_pair(in3[p], in3[p + 1], m, w1_ref)
        for j in range(2):
            e = 1 + 2 * p + j
            a = out[:, j * C : (j + 1) * C]
            if DEPTH <= e < DEPTH + SLOTS:
                pre_s[m, e - DEPTH] = a
            half = jnp.where(outside(e), 0.0, 0.5)
            put3(hid3[p], m, j, (a * half) * (1.0 + jnp.tanh(0.5 * a)))

    def make_forecast(m, p):
        out = conv_pair(hid3[p], hid3[p + 1], m, w2_ref)
        for j in range(2):
            v = in3[p + 1][m, j, :, C : 2 * C].astype(F32) + out[:, j * C : (j + 1) * C]
            fc_s[m, 2 * p + j] = v.astype(BF)

    def member(m, _):
        make_inputs(m, 0)
        make_inputs(m, 1)
        make_inputs(m, 2)
        make_hidden(m, 0)
        make_inputs(m, 3)
        make_hidden(m, 1)
        make_inputs(m, 4)
        make_forecast(m, 0)
        make_hidden(m, 2)
        make_forecast(m, 1)
        make_hidden(m, 3)
        make_forecast(m, 2)
        return 0

    lax.fori_loop(0, MEM, member, 0)

    pair_scale = 1.0 / (MEM * (MEM - 1))
    factor = 1.0 / math.sqrt(ROWS_TOTAL * LON)

    step = 32

    def make_crps(r, loss):
        e = r + 2
        g = jnp.clip(offset - DEPTH + e, 0, ROWS_TOTAL - 1)
        weight = jnp.where(outside(e), 0.0, weight_ref[g])
        mine = ((r >= 1) & (r < 1 + n)).astype(F32)
        scale = weight * (factor * pair_scale)
        slot = jnp.clip(r - 1, 0, SLOTS - 1)

        def chunk(k, _):
            at = pl.ds(pl.multiple_of(k * step, step), step)
            t = tgt_s[r, at].astype(F32)
            f = [fc_s[m, r, at].astype(F32) for m in range(MEM)]
            skill = None
            spread = None
            slopes = []
            for m in range(MEM):
                d = f[m] - t
                q = d * d + SMOOTH
                inv = lax.rsqrt(q)
                skill = q * inv if skill is None else skill + q * inv
                slopes.append(d * inv * (MEM - 1.0))
            for a in range(MEM):
                for b in range(a + 1, MEM):
                    d = f[a] - f[b]
                    q = d * d + SMOOTH
                    inv = lax.rsqrt(q)
                    spread = q * inv if spread is None else spread + q * inv
                    tilt = d * inv
                    slopes[a] = slopes[a] - tilt
                    slopes[b] = slopes[b] + tilt
            crps_s[at] = (skill * (MEM - 1.0) - spread) * pair_scale
            for m in range(MEM):
                cbuf_s[m, pl.ds(pl.multiple_of(PAD + k * step, 8), step)] = slopes[m] * scale
            return 0

        lax.fori_loop(0, J // step, chunk, 0)
        for m in range(MEM):
            mid = cbuf_s[m, PAD : PAD + J]
            cot3_s[m, r, :, C : 2 * C] = mid.astype(BF)
            cot3_s[m, r, :, 0:C] = cbuf_s[m, PAD - 1 : PAD - 1 + J].astype(BF)
            cot3_s[m, r, :, 2 * C :] = cbuf_s[m, PAD + 1 : PAD + 1 + J].astype(BF)

        @pl.when((r >= 1) & (r < 1 + SLOTS))
        def _():
            for m in range(MEM):
                ya_s[m, slot] = cot3_s[m, r, :, C : 2 * C]
                trim(ya_s, m, slot)
            @pl.when(r > n)
            def _():
                ya_s[:, slot] = jnp.zeros((MEM, J, C), BF)

            cells_ref[slot] = jnp.sum(jnp.transpose(crps_s[...]), axis=0, keepdims=True) * (
                weight * mine * (1.0 / C)
            )

        return loss

    for m in range(MEM):
        cbuf_s[m, 0:PAD] = jnp.zeros((PAD, C), F32)
        cbuf_s[m, PAD + J :] = jnp.zeros((PAD, C), F32)
    lax.fori_loop(0, SLOTS + 2, make_crps, 0)
    loss = cells_ref[0] + cells_ref[1] + cells_ref[2] + cells_ref[3]
    lane = lax.broadcasted_iota(jnp.int32, (1, J), 1)
    loss = jnp.where((lane >= LEFT) & (lane < LEFT + OWN), loss, 0.0)

    def make_pre_cot(i, _):
        p, m = i // MEM, i % MEM
        lhs = jnp.concatenate([cot3_s[m, 2 * p + r] for r in range(4)], axis=1)
        out = jnp.dot(lhs, wt_ref[...], preferred_element_type=F32)
        for k in range(2):
            s = 2 * p + k
            a = pre_s[m, s]
            t = jnp.tanh(0.5 * a)
            mine = jnp.where(s < n, 0.25, 0.0)
            v = out[:, k * C : (k + 1) * C] * (((1.0 + t) * mine) * (2.0 + a * (1.0 - t)))
            yb_s[m, s] = v.astype(BF)
            trim(yb_s, m, s)
        return 0

    lax.fori_loop(0, 2 * MEM, make_pre_cot, 0)

    def weight_grad(rows, y, slot):
        acc_s[...] = jnp.zeros_like(acc_s)

        def step(m, _):
            ys = jnp.concatenate(
                [
                    jnp.concatenate([y[m, 0], y[m, 1]], axis=1),
                    jnp.concatenate([y[m, 2], y[m, 3]], axis=1),
                ],
                axis=0,
            )
            xs = jnp.concatenate(
                [
                    jnp.concatenate([ref[m, j] for ref, j in rows[a : a + 4]], axis=1)
                    for a in (0, 2)
                ],
                axis=0,
            )
            acc_s[...] += lax.dot_general(
                ys, xs, (((0,), (0,)), ((), ())), preferred_element_type=F32
            )
            return 0

        lax.fori_loop(0, MEM, step, 0)
        biggest = jnp.zeros((C, C), F32)
        for k in range(9):
            blk = acc_s[0:C, k * C : (k + 1) * C] + acc_s[C:, 384 + k * C : 384 + (k + 1) * C]
            biggest = jnp.maximum(biggest, jnp.abs(blk))
            grads_ref[slot, k * C : (k + 1) * C] = jnp.transpose(blk)
        return biggest

    top1 = weight_grad([(in3[e // 2], e % 2) for e in range(2, 8)], yb_s, core)
    top2 = weight_grad([(hid3[(e - 1) // 2], (e - 1) % 2) for e in range(2, 8)], ya_s, 1 - core)
    biggest = jnp.max(jnp.max(jnp.maximum(top1, top2), axis=0, keepdims=True), axis=1, keepdims=True)
    loss = jnp.sum(loss, axis=1, keepdims=True) * (1.0 / (ROWS_TOTAL * LON))
    for slot in range(2):
        grads_ref[slot, G : G + 1] = jnp.broadcast_to(biggest, (1, C))
        grads_ref[slot, G + 1 : G + 2] = jnp.broadcast_to(loss, (1, C))
        grads_ref[slot, G + 2 :] = jnp.zeros((6, C), F32)


def local_step(counts, seeds, place, weights, state, target, mine, other, amp, w1, w2, wt):
    smem = pl.BlockSpec(memory_space=pltpu.SMEM)
    vmem = pl.BlockSpec(memory_space=pltpu.VMEM)
    hbm = pl.BlockSpec(memory_space=pl.ANY)
    return pl.pallas_call(
        kernel,
        out_shape=(
            jax.ShapeDtypeStruct((2, G + 8, C), F32),
            jax.ShapeDtypeStruct((SLOTS, 1, J), F32),
        ),
        in_specs=[smem] * 4 + [hbm] * 2 + [vmem] * 6,
        out_specs=(vmem, vmem),
        scratch_shapes=[
            pltpu.VMEM((EXT, J, C), BF),
            pltpu.VMEM((SLOTS + 2, J, C), BF),
            pltpu.VMEM((J, C), jnp.int32),
            [pltpu.VMEM((J + 2 * PAD, C), F32) for _ in range(6)],
            pltpu.VMEM((MEM, J + 2 * PAD, C), F32),
            pltpu.VMEM((J, C), F32),
            [pltpu.VMEM((MEM + (k < 3), 2, J, 3 * C), BF) for k in range(5)],
            [pltpu.VMEM((MEM, 2, J, 3 * C), BF) for _ in range(4)],
            pltpu.VMEM((MEM, EXT - 4, J, 3 * C), BF),
            pltpu.VMEM((MEM, SLOTS, J, C), F32),
            pltpu.VMEM((MEM, EXT - 4, J, C), BF),
            pltpu.VMEM((MEM, SLOTS, J, C), BF),
            pltpu.VMEM((MEM, SLOTS, J, C), BF),
            pltpu.VMEM((2 * C, 4 * 384), F32),
            pltpu.SemaphoreType.DMA((2, 2)),
        ],
        compiler_params=pltpu.CompilerParams(vmem_limit_bytes=60 * 1024 * 1024),
        name="ensemble_step",
    )(counts, seeds, place, weights, state, target, mine, other, amp, w1, w2, wt)


def paired(filt):
    flat = filt.reshape(9 * C, C)
    return jnp.concatenate(
        [jnp.pad(flat, ((0, 3 * C), (0, 0))), jnp.pad(flat, ((3 * C, 0), (0, 0)))], axis=1
    )


def body(state, target, amp, filt1, filt2, counts, seed):
    band = lax.axis_index("band")
    member = lax.axis_index("member")
    core = member % 2
    weights = jnp.asarray(
        np.cos(np.pi * ((np.arange(ROWS_TOTAL) + 0.5) / GRID_ROWS - 0.5)).astype(np.float32)
    )
    place = jnp.stack([band, member]).astype(jnp.int32)
    seeds = jnp.where(jnp.arange(MEM) == member, seed, 0)
    seeds = seeds + shift(seeds, 4, 1)
    one, two, three, flags = edges(counts, place, state, target)

    def send(value, by):
        pairs = [(i, (i // 4 + by * (1 - 2 * (i % 2))) % 32 * 4 + i % 4) for i in range(128)]
        return lax.ppermute(value, BM, pairs)

    def flag(k):
        return flags[k : k + 1][None] > 0.5

    one, seeds = lax.optimization_barrier((one, seeds))
    g1 = send(one, 1)
    seeds = seeds + shift(seeds, 3, 1)
    two, three, seeds = lax.optimization_barrier((two, three, seeds))
    g2 = send(two, 2)
    g3 = send(three, 3)
    row2 = jnp.where(flag(0), g1[1:2], g2[:1])
    row3 = jnp.where(
        flag(1), g1[2:3], jnp.where(flag(2), g2[:1], jnp.where(flag(3), g2[1:], g3))
    )
    halo = jnp.concatenate([g1[:1], row2, row3, g1[3:]], axis=0)
    mine = lax.dynamic_slice_in_dim(halo, OWN * core, J, 1)
    other = shift(lax.dynamic_slice_in_dim(halo, OWN * (1 - core), J, 1), 4, 1)

    w1 = paired(filt1)
    w2 = paired(filt2)
    wt = paired(jnp.transpose(filt2[::-1, ::-1], (0, 1, 3, 2)))
    grads, cells = local_step(
        counts, seeds, place, weights, state, target, mine, other, amp[None], w1, w2, wt
    )

    mean_loss, grad_one, grad_two = reduce_all(grads[0], grads[1], band, member)
    return cells[:, 0, LEFT : LEFT + OWN], mean_loss, grad_one, grad_two


def solution(mesh):
    in_specs = (P("band", None, None), P("band", None, None), P(), P(), P(), P(), P("member"))
    out_specs = (P("band", "member"), P(), P(), P())
    return jax.shard_map(body, mesh=mesh, in_specs=in_specs, out_specs=out_specs, check_vma=False)
```

```python
import math

import jax
import jax.numpy as jnp
import numpy as np
from jax import lax
from jax.experimental import pallas as pl
from jax.experimental.pallas import tpu as pltpu
from jax.sharding import PartitionSpec as P

GRID_ROWS = 721
HALF = 720
ROWS_TOTAL = 96
SMOOTH = 0.01
LON = 1440
OWN = 360
LEFT = 8
J = 384
C = 128
MEM = 4
SLOTS = 4
DEPTH = 3
EXT = SLOTS + 2 * DEPTH
PAD = 8
W = 752
G = 1152
TAIL = 16
BF = jnp.bfloat16
F32 = jnp.float32
BM = ("band", "member")


def coords(i):
    return [i // 64, i // 16 % 4, i // 4 % 4, i // 2 % 2, i % 2]


def index(v):
    return (((v[0] * 4 + v[1]) * 4 + v[2]) * 2 + v[3]) * 2 + v[4]


SIZES = [2, 4, 4, 2, 2]


def permute(value, move):
    return lax.ppermute(value, BM, [(i, index(move(coords(i)))) for i in range(128)])


def shift(value, dim, by):
    def move(v):
        v[dim] = (v[dim] + by) % SIZES[dim]
        return v

    return permute(value, move)


def shift_z(value, by):
    def move(v):
        z = (2 * v[3] + v[0] + by) % 4
        v[3], v[0] = z // 2, z % 2
        return v

    return permute(value, move)


def root(bound):
    return half(jnp.sqrt(jnp.maximum(bound, 2.0**-24)) * 1.001)


def half(value):
    return lax.reduce_precision(value, exponent_bits=5, mantissa_bits=10)


def encode(value, bound, loss):
    r = root(bound)
    q = (value * (1.0 / (r * r))).astype(jnp.float16)
    rl = root(jnp.abs(loss))
    share = loss * (1.0 / (rl * rl))
    high = half(share)
    low = (share - high) * 1024.0
    tail = jnp.concatenate([r, rl, high, low, jnp.zeros((TAIL - 4, C), F32)], axis=0)
    return q, tail.astype(jnp.float16)


def decode(message):
    q, tail = message[:-TAIL].astype(F32), message[-TAIL:].astype(F32)
    r, rl = tail[0:1], tail[1:2]
    scale = r * r
    return q * scale, scale, (tail[2:3] + tail[3:4] * (1.0 / 1024.0)) * (rl * rl)


def ordered(own, got, place):
    out = jnp.zeros((len(got) + 1,) + own.shape, own.dtype)
    out = lax.dynamic_update_index_in_dim(out, own, place, 0)
    for d, g in enumerate(got, 1):
        out = lax.dynamic_update_index_in_dim(out, g, (place - d) % (len(got) + 1), 0)
    return out


def total(messages):
    parts = [decode(messages[k]) for k in range(messages.shape[0])]
    value, bound, loss = parts[0]
    for v, b, l in parts[1:]:
        value, bound, loss = value + v, bound + b, loss + l
    return value, bound, loss


def reduce_all(kept, sent, band, member):
    core = member % 2
    x, y = band % 4, band // 4 % 4
    z = 2 * (member // 2) + band // 16
    got = shift(sent, 4, 1)
    value = kept[:G] + got[:G]
    bound = kept[G : G + 1] + got[G : G + 1]
    loss = kept[G + 1 : G + 2] + got[G + 1 : G + 2]

    q, tail = encode(value, bound, loss)
    parts = q.reshape(4, G // 4, C)

    def part(k):
        return jnp.concatenate([lax.dynamic_index_in_dim(parts, k, 0, keepdims=False), tail], axis=0)

    got = [shift(part((x + d) % 4), 2, d) for d in range(1, 4)]
    value, bound, loss = total(ordered(part(x), got, x))

    message = jnp.concatenate(encode(value, bound, loss), axis=0)
    value, bound, loss = total(ordered(message, [shift(message, 1, d) for d in range(1, 4)], y))

    message = jnp.concatenate(encode(value, bound, loss), axis=0)
    value, bound, loss = total(ordered(message, [shift_z(message, d) for d in range(1, 4)], z))

    message = jnp.concatenate(encode(value, bound, loss), axis=0)
    messages = ordered(message, [shift(message, 2, d) for d in range(1, 4)], x)
    value = jnp.concatenate([decode(messages[k])[0] for k in range(4)], axis=0)
    other = shift(value, 4, 1)
    first = jnp.where(core == 0, value, other)
    second = jnp.where(core == 0, other, value)
    return loss[0, 0], first.reshape(3, 3, C, C), second.reshape(3, 3, C, C)


def chip_row(half, src, r, dst, sem):
    cut = LON - (HALF - LEFT)
    left = [
        pltpu.make_async_copy(src.at[r, pl.ds(LON - LEFT, LEFT)], dst.at[pl.ds(0, LEFT)], sem.at[0]),
        pltpu.make_async_copy(
            src.at[r, pl.ds(0, W - LEFT)], dst.at[pl.ds(LEFT, W - LEFT)], sem.at[1]
        ),
    ]
    right = [
        pltpu.make_async_copy(src.at[r, pl.ds(HALF - LEFT, cut)], dst.at[pl.ds(0, cut)], sem.at[0]),
        pltpu.make_async_copy(src.at[r, pl.ds(0, W - cut)], dst.at[pl.ds(cut, W - cut)], sem.at[1]),
    ]
    return [(half == 0, left), (half == 1, right)]


def own_window(quarter, src, dst, sem):
    cut = LON - (3 * OWN - LEFT)
    middle = pl.multiple_of(quarter * OWN - LEFT, 8)
    first = [
        pltpu.make_async_copy(
            src.at[:, pl.ds(LON - LEFT, LEFT)], dst.at[:, pl.ds(0, LEFT)], sem.at[0]
        ),
        pltpu.make_async_copy(
            src.at[:, pl.ds(0, J - LEFT)], dst.at[:, pl.ds(LEFT, J - LEFT)], sem.at[1]
        ),
    ]
    inner = [pltpu.make_async_copy(src.at[:, pl.ds(middle, J)], dst, sem.at[0])]
    last = [
        pltpu.make_async_copy(
            src.at[:, pl.ds(3 * OWN - LEFT, cut)], dst.at[:, pl.ds(0, cut)], sem.at[0]
        ),
        pltpu.make_async_copy(
            src.at[:, pl.ds(0, J - cut)], dst.at[:, pl.ds(cut, J - cut)], sem.at[1]
        ),
    ]
    return [(quarter == 0, first), ((quarter == 1) | (quarter == 2), inner), (quarter == 3, last)]


def start(cases):
    for cond, copies in cases:

        @pl.when(cond)
        def _():
            for c in copies:
                c.start()


def wait(cases):
    for cond, copies in cases:

        @pl.when(cond)
        def _():
            for c in copies:
                c.wait()


def edge_kernel(counts_ref, place_ref, state_ref, target_ref, one_ref, two_ref, three_ref, flag_ref, sem):
    band = place_ref[0]
    member = place_ref[1]
    half, core = member // 2, member % 2
    n = counts_ref[band]
    back = 2 * core - 1
    near = counts_ref[jnp.clip(band + back, 0, 31)]
    far = counts_ref[jnp.clip(band + 2 * back, 0, 31)]
    row = lambda k: jnp.where(core == 0, jnp.maximum(n - 1 - k, 0), k)
    sends = [(state_ref, 0, one_ref, 0), (state_ref, 1, one_ref, 1), (state_ref, 2, one_ref, 2)]
    sends += [(target_ref, 0, one_ref, 3)]
    sends += [(state_ref, 0, two_ref, 0), (state_ref, 1, two_ref, 1), (state_ref, 0, three_ref, 0)]
    cases = []
    for i, (src, k, dst, slot) in enumerate(sends):
        cases += chip_row(half, src, row(k), dst.at[slot], sem.at[i])
    start(cases)
    ones = jnp.ones((1, C), F32)
    flag_ref[0:1] = ones * (near >= 2).astype(F32)
    flag_ref[1:2] = ones * (near >= 3).astype(F32)
    flag_ref[2:3] = ones * (near == 2).astype(F32)
    flag_ref[3:4] = ones * (far >= 2).astype(F32)
    flag_ref[4:8] = jnp.zeros((4, C), F32)
    wait(cases)


def edges(counts, place, state, target):
    smem = pl.BlockSpec(memory_space=pltpu.SMEM)
    vmem = pl.BlockSpec(memory_space=pltpu.VMEM)
    hbm = pl.BlockSpec(memory_space=pl.ANY)
    rows = lambda k: jax.ShapeDtypeStruct((k, W, C), BF)
    return pl.pallas_call(
        edge_kernel,
        out_shape=(rows(4), rows(2), rows(1), jax.ShapeDtypeStruct((8, C), F32)),
        in_specs=[smem, smem, hbm, hbm],
        out_specs=(vmem,) * 4,
        scratch_shapes=[pltpu.SemaphoreType.DMA((7, 2))],
        name="edge_rows",
    )(counts, place, state, target)


def kernel(
    counts_ref, seeds_ref, place_ref, weight_ref,
    state_ref, target_ref, mine_ref, other_ref,
    amp_ref, w1_ref, w2_ref, wt_ref,
    grads_ref, cells_ref,
    state_s, tgt_s, hash_s, bufs, cbuf_s, crps_s,
    in3, hid3, cot3_s, pre_s, fc_s, ya_s, yb_s, acc_s, acc2_s, sem,
):
    band = place_ref[0]
    quarter = place_ref[1]
    core = quarter % 2
    n = counts_ref[band]
    offset = lax.fori_loop(0, band, lambda b, s: s + counts_ref[b], jnp.int32(0))

    copies = own_window(quarter, state_ref, state_s.at[pl.ds(DEPTH, SLOTS)], sem.at[0])
    copies += own_window(quarter, target_ref, tgt_s.at[pl.ds(1, SLOTS)], sem.at[1])
    start(copies)

    for buf in bufs:
        buf[0:PAD] = jnp.zeros((PAD, C), F32)
        buf[PAD + J :] = jnp.zeros((PAD, C), F32)

    cols = lax.broadcasted_iota(jnp.int32, (J, C), 0)
    chan = lax.broadcasted_iota(jnp.int32, (J, C), 1)
    lon = quarter * OWN - LEFT + cols
    lon = jnp.where(lon < 0, lon + LON, jnp.where(lon >= LON, lon - LON, lon))
    hash_s[...] = lon * 668265263 + chan * 1274126177

    wait(copies)

    def put_edges(above, below):
        for slot, k in ((2, 0), (1, 1), (0, 2)):
            state_s[slot] = above[k]
        for slot, k in ((0, 0), (1, 1), (2, 2)):
            state_s[DEPTH + n + slot] = below[k]
        tgt_s[0] = above[3]
        tgt_s[1 + n] = below[3]

    @pl.when(core == 0)
    def _():
        put_edges(mine_ref, other_ref)

    @pl.when(core == 1)
    def _():
        put_edges(other_ref, mine_ref)

    def outside(e):
        g = offset - DEPTH + e
        return (g < 0) | (g >= ROWS_TOTAL)

    def trim(ref, m, slot):
        ref[m, slot, 0:LEFT] = jnp.zeros((LEFT, C), BF)
        ref[m, slot, LEFT + OWN :] = jnp.zeros((J - OWN - LEFT, C), BF)

    for e in (0, 1, 2):

        @pl.when(outside(e))
        def _():
            state_s[e] = jnp.zeros((J, C), BF)

    for e in range(DEPTH + 1, EXT):

        @pl.when(outside(e))
        def _():
            state_s[e] = jnp.zeros((J, C), BF)

    turn = [0]

    def put3(ref, m, slot, v):
        buf = bufs[turn[0] % len(bufs)]
        turn[0] += 1
        buf[PAD : PAD + J] = v
        ref[m, slot, :, C : 2 * C] = v.astype(BF)
        ref[m, slot, :, 0:C] = buf[PAD - 1 : PAD - 1 + J].astype(BF)
        ref[m, slot, :, 2 * C :] = buf[PAD + 1 : PAD + 1 + J].astype(BF)

    amp = amp_ref[...]
    amp_step = amp * (1.0 / 32768.0)
    amp_base = amp * (0.5 / 32768.0 - 1.0)

    def make_inputs(m, k):
        seed = seeds_ref[m] * 1103515245
        for j in range(2):
            e = 2 * k + j
            live = jnp.where(outside(e), 0.0, 1.0)
            h = hash_s[...] + ((offset - DEPTH + e) * 374761393 + seed)
            h = h ^ (h >> 13)
            h = h * 1274126177
            h = h ^ (h >> 16)
            v = (state_s[e].astype(F32) + amp_base * live) + (h & 65535).astype(F32) * (
                amp_step * live
            )
            put3(in3[k], m, j, v)

    def conv_pair(top, bottom, m, w):
        lhs = jnp.concatenate([top[m, 0], top[m, 1], bottom[m, 0], bottom[m, 1]], axis=1)
        return jnp.dot(lhs, w[...], preferred_element_type=F32)

    def make_hidden(m, p):
        out = conv_pair(in3[p], in3[p + 1], m, w1_ref)
        for j in range(2):
            e = 1 + 2 * p + j
            a = out[:, j * C : (j + 1) * C]
            if DEPTH <= e < DEPTH + SLOTS:
                pre_s[m, e - DEPTH] = a
            half = jnp.where(outside(e), 0.0, 0.5)
            put3(hid3[p], m, j, (a * half) * (1.0 + jnp.tanh(0.5 * a)))

    def make_forecast(m, p):
        out = conv_pair(hid3[p], hid3[p + 1], m, w2_ref)
        for j in range(2):
            v = in3[p + 1][m, j, :, C : 2 * C].astype(F32) + out[:, j * C : (j + 1) * C]
            fc_s[m, 2 * p + j] = v.astype(BF)

    def member(m, _):
        make_inputs(m, 0)
        make_inputs(m, 1)
        make_inputs(m, 2)
        make_hidden(m, 0)
        make_inputs(m, 3)
        make_hidden(m, 1)
        make_inputs(m, 4)
        make_forecast(m, 0)
        make_hidden(m, 2)
        make_forecast(m, 1)
        make_hidden(m, 3)
        make_forecast(m, 2)
        return 0

    lax.fori_loop(0, MEM, member, 0)

    pair_scale = 1.0 / (MEM * (MEM - 1))
    factor = 1.0 / math.sqrt(ROWS_TOTAL * LON)

    step = 32

    def crps_chunk(r, k, scale):
        at = pl.ds(k * step, step)
        if not isinstance(k, int):
            at = pl.ds(pl.multiple_of(k * step, step), step)
        t = tgt_s[r, at].astype(F32)
        f = [fc_s[m, r, at].astype(F32) for m in range(MEM)]
        skill = None
        spread = None
        slopes = []
        for m in range(MEM):
            d = f[m] - t
            q = d * d + SMOOTH
            inv = lax.rsqrt(q)
            skill = q * inv if skill is None else skill + q * inv
            slopes.append(d * inv * (MEM - 1.0))
        for a in range(MEM):
            for b in range(a + 1, MEM):
                d = f[a] - f[b]
                q = d * d + SMOOTH
                inv = lax.rsqrt(q)
                spread = q * inv if spread is None else spread + q * inv
                tilt = d * inv
                slopes[a] = slopes[a] - tilt
                slopes[b] = slopes[b] + tilt
        crps_s[at] = (skill * (MEM - 1.0) - spread) * pair_scale
        for m in range(MEM):
            start_at = PAD + k * step
            if not isinstance(k, int):
                start_at = pl.multiple_of(start_at, 8)
            cbuf_s[m, pl.ds(start_at, step)] = slopes[m] * scale

    def crps_weight(r):
        g = jnp.clip(offset - DEPTH + 2 + r, 0, ROWS_TOTAL - 1)
        return jnp.where(outside(r + 2), 0.0, weight_ref[g])

    def spread_out(r):
        for m in range(MEM):
            cot3_s[m, r, :, C : 2 * C] = cbuf_s[m, PAD : PAD + J].astype(BF)
            cot3_s[m, r, :, 0:C] = cbuf_s[m, PAD - 1 : PAD - 1 + J].astype(BF)
            cot3_s[m, r, :, 2 * C :] = cbuf_s[m, PAD + 1 : PAD + 1 + J].astype(BF)

    def keep_own(r, weight):
        for m in range(MEM):
            ya_s[m, r - 1] = jnp.where(r > n, 0.0, cbuf_s[m, PAD : PAD + J]).astype(BF)
            trim(ya_s, m, r - 1)
        mine = jnp.where(r > n, 0.0, weight * (1.0 / C))
        cells_ref[r - 1] = jnp.sum(jnp.transpose(crps_s[...]), axis=0, keepdims=True) * mine

    def crps_row(r):
        weight = crps_weight(r)
        for k in range(J // step):
            crps_chunk(r, k, weight * (factor * pair_scale))
        spread_out(r)
        if 1 <= r <= SLOTS:
            keep_own(r, weight)

    for m in range(MEM):
        cbuf_s[m, 0:PAD] = jnp.zeros((PAD, C), F32)
        cbuf_s[m, PAD + J :] = jnp.zeros((PAD, C), F32)

    def crps_looped(r, _):
        weight = crps_weight(r)

        def chunk(k, _):
            crps_chunk(r, k, weight * (factor * pair_scale))
            return 0

        lax.fori_loop(0, J // step, chunk, 0)
        spread_out(r)

        @pl.when(r >= 1)
        def _():
            keep_own(r, weight)

        return 0

    lax.fori_loop(0, 3, crps_looped, 0)

    def make_pre_cot(m, p):
        lhs = jnp.concatenate([cot3_s[m, 2 * p + r] for r in range(4)], axis=1)
        out = jnp.dot(lhs, wt_ref[...], preferred_element_type=F32)
        for k in range(2):
            s = 2 * p + k
            a = pre_s[m, s]
            t = jnp.tanh(0.5 * a)
            mine = jnp.where(s < n, 0.25, 0.0)
            v = out[:, k * C : (k + 1) * C] * (((1.0 + t) * mine) * (2.0 + a * (1.0 - t)))
            yb_s[m, s] = v.astype(BF)
            trim(yb_s, m, s)

    hidden_rows = [(hid3[(e - 1) // 2], (e - 1) % 2) for e in range(2, 8)]

    def grad_two(p):
        for g in (0, 2):
            ys = jnp.concatenate(
                [jnp.concatenate([ya_s[m, 2 * p], ya_s[m, 2 * p + 1]], axis=1) for m in (g, g + 1)],
                axis=0,
            )
            xs = jnp.concatenate(
                [
                    jnp.concatenate([ref[m, j] for ref, j in hidden_rows[2 * p : 2 * p + 4]], axis=1)
                    for m in (g, g + 1)
                ],
                axis=0,
            )
            part = lax.dot_general(ys, xs, (((0,), (0,)), ((), ())), preferred_element_type=F32)
            if p == 0 and g == 0:
                acc2_s[...] = part
            else:
                acc2_s[...] += part

    crps_row(3)
    grad_two(0)
    crps_row(4)
    for m in range(MEM):
        make_pre_cot(m, 0)
    crps_row(5)
    grad_two(1)
    for m in range(MEM):
        make_pre_cot(m, 1)
    loss = cells_ref[0] + cells_ref[1] + cells_ref[2] + cells_ref[3]
    lane = lax.broadcasted_iota(jnp.int32, (1, J), 1)
    loss = jnp.where((lane >= LEFT) & (lane < LEFT + OWN), loss, 0.0)

    def accumulate(rows, y):
        acc_s[...] = jnp.zeros_like(acc_s)

        def step(m, _):
            ys = jnp.concatenate(
                [
                    jnp.concatenate([y[m, 0], y[m, 1]], axis=1),
                    jnp.concatenate([y[m, 2], y[m, 3]], axis=1),
                ],
                axis=0,
            )
            xs = jnp.concatenate(
                [
                    jnp.concatenate([ref[m, j] for ref, j in rows[a : a + 4]], axis=1)
                    for a in (0, 2)
                ],
                axis=0,
            )
            acc_s[...] += lax.dot_general(
                ys, xs, (((0,), (0,)), ((), ())), preferred_element_type=F32
            )
            return 0

        lax.fori_loop(0, MEM, step, 0)

    def finish(acc, slot):
        biggest = jnp.zeros((C, C), F32)
        for k in range(9):
            blk = acc[0:C, k * C : (k + 1) * C] + acc[C:, 384 + k * C : 384 + (k + 1) * C]
            biggest = jnp.maximum(biggest, jnp.abs(blk))
            grads_ref[slot, k * C : (k + 1) * C] = jnp.transpose(blk)
        return biggest

    top2 = finish(acc2_s, 1 - core)
    accumulate([(in3[e // 2], e % 2) for e in range(2, 8)], yb_s)
    top1 = finish(acc_s, core)
    biggest = jnp.max(jnp.max(jnp.maximum(top1, top2), axis=0, keepdims=True), axis=1, keepdims=True)
    loss = jnp.sum(loss, axis=1, keepdims=True) * (1.0 / (ROWS_TOTAL * LON))
    for slot in range(2):
        grads_ref[slot, G : G + 1] = jnp.broadcast_to(biggest, (1, C))
        grads_ref[slot, G + 1 : G + 2] = jnp.broadcast_to(loss, (1, C))
        grads_ref[slot, G + 2 :] = jnp.zeros((6, C), F32)


def local_step(counts, seeds, place, weights, state, target, mine, other, amp, w1, w2, wt):
    smem = pl.BlockSpec(memory_space=pltpu.SMEM)
    vmem = pl.BlockSpec(memory_space=pltpu.VMEM)
    hbm = pl.BlockSpec(memory_space=pl.ANY)
    return pl.pallas_call(
        kernel,
        out_shape=(
            jax.ShapeDtypeStruct((2, G + 8, C), F32),
            jax.ShapeDtypeStruct((SLOTS, 1, J), F32),
        ),
        in_specs=[smem] * 4 + [hbm] * 2 + [vmem] * 6,
        out_specs=(vmem, vmem),
        scratch_shapes=[
            pltpu.VMEM((EXT, J, C), BF),
            pltpu.VMEM((SLOTS + 2, J, C), BF),
            pltpu.VMEM((J, C), jnp.int32),
            [pltpu.VMEM((J + 2 * PAD, C), F32) for _ in range(6)],
            pltpu.VMEM((MEM, J + 2 * PAD, C), F32),
            pltpu.VMEM((J, C), F32),
            [pltpu.VMEM((MEM, 2, J, 3 * C), BF) for _ in range(5)],
            [pltpu.VMEM((MEM, 2, J, 3 * C), BF) for _ in range(4)],
            pltpu.VMEM((MEM, EXT - 4, J, 3 * C), BF),
            pltpu.VMEM((MEM, SLOTS, J, C), F32),
            pltpu.VMEM((MEM, EXT - 4, J, C), BF),
            pltpu.VMEM((MEM, SLOTS, J, C), BF),
            pltpu.VMEM((MEM, SLOTS, J, C), BF),
            pltpu.VMEM((2 * C, 4 * 384), F32),
            pltpu.VMEM((2 * C, 4 * 384), F32),
            pltpu.SemaphoreType.DMA((2, 2)),
        ],
        compiler_params=pltpu.CompilerParams(vmem_limit_bytes=60 * 1024 * 1024),
        name="ensemble_step",
    )(counts, seeds, place, weights, state, target, mine, other, amp, w1, w2, wt)


def paired(filt):
    flat = filt.reshape(9 * C, C)
    return jnp.concatenate(
        [jnp.pad(flat, ((0, 3 * C), (0, 0))), jnp.pad(flat, ((3 * C, 0), (0, 0)))], axis=1
    )


def body(state, target, amp, filt1, filt2, counts, seed):
    band = lax.axis_index("band")
    member = lax.axis_index("member")
    core = member % 2
    weights = jnp.asarray(
        np.cos(np.pi * ((np.arange(ROWS_TOTAL) + 0.5) / GRID_ROWS - 0.5)).astype(np.float32)
    )
    place = jnp.stack([band, member]).astype(jnp.int32)
    seeds = jnp.where(jnp.arange(MEM) == member, seed, 0)
    seeds = seeds + shift(seeds, 4, 1)
    one, two, three, flags = edges(counts, place, state, target)

    def send(value, by):
        pairs = [(i, (i // 4 + by * (1 - 2 * (i % 2))) % 32 * 4 + i % 4) for i in range(128)]
        return lax.ppermute(value, BM, pairs)

    def flag(k):
        return flags[k : k + 1][None] > 0.5

    one, seeds = lax.optimization_barrier((one, seeds))
    g1 = send(one, 1)
    seeds = seeds + shift(seeds, 3, 1)
    two, three, seeds = lax.optimization_barrier((two, three, seeds))
    g2 = send(two, 2)
    g3 = send(three, 3)
    row2 = jnp.where(flag(0), g1[1:2], g2[:1])
    row3 = jnp.where(
        flag(1), g1[2:3], jnp.where(flag(2), g2[:1], jnp.where(flag(3), g2[1:], g3))
    )
    halo = jnp.concatenate([g1[:1], row2, row3, g1[3:]], axis=0)
    mine = lax.dynamic_slice_in_dim(halo, OWN * core, J, 1)
    other = shift(lax.dynamic_slice_in_dim(halo, OWN * (1 - core), J, 1), 4, 1)

    w1 = paired(filt1)
    w2 = paired(filt2)
    wt = paired(jnp.transpose(filt2[::-1, ::-1], (0, 1, 3, 2)))
    grads, cells = local_step(
        counts, seeds, place, weights, state, target, mine, other, amp[None], w1, w2, wt
    )

    mean_loss, grad_one, grad_two = reduce_all(grads[0], grads[1], band, member)
    return cells[:, 0, LEFT : LEFT + OWN], mean_loss, grad_one, grad_two


def solution(mesh):
    in_specs = (P("band", None, None), P("band", None, None), P(), P(), P(), P(), P("member"))
    out_specs = (P("band", "member"), P(), P(), P())
    return jax.shard_map(body, mesh=mesh, in_specs=in_specs, out_specs=out_specs, check_vma=False)
```

```python
import math

import jax
import jax.numpy as jnp
import numpy as np
from jax import lax
from jax.experimental import pallas as pl
from jax.experimental.pallas import tpu as pltpu
from jax.sharding import PartitionSpec as P

GRID_ROWS = 721
HALF = 720
ROWS_TOTAL = 96
SMOOTH = 0.01
LON = 1440
OWN = 360
LEFT = 8
J = 384
C = 128
MEM = 4
SLOTS = 4
DEPTH = 3
EXT = SLOTS + 2 * DEPTH
PAD = 8
W = 752
G = 1152
TAIL = 16
BF = jnp.bfloat16
F32 = jnp.float32
BM = ("band", "member")


def coords(i):
    return [i // 64, i // 16 % 4, i // 4 % 4, i // 2 % 2, i % 2]


def index(v):
    return (((v[0] * 4 + v[1]) * 4 + v[2]) * 2 + v[3]) * 2 + v[4]


SIZES = [2, 4, 4, 2, 2]


def permute(value, move):
    return lax.ppermute(value, BM, [(i, index(move(coords(i)))) for i in range(128)])


def shift(value, dim, by):
    def move(v):
        v[dim] = (v[dim] + by) % SIZES[dim]
        return v

    return permute(value, move)


def shift_z(value, by):
    def move(v):
        z = (2 * v[3] + v[0] + by) % 4
        v[3], v[0] = z // 2, z % 2
        return v

    return permute(value, move)


def root(bound):
    return half(jnp.sqrt(jnp.maximum(bound, 2.0**-24)) * 1.001)


def half(value):
    return lax.reduce_precision(value, exponent_bits=5, mantissa_bits=10)


def encode(value, bound, loss):
    r = root(bound)
    q = (value * (1.0 / (r * r))).astype(jnp.float16)
    rl = root(jnp.abs(loss))
    share = loss * (1.0 / (rl * rl))
    high = half(share)
    low = (share - high) * 1024.0
    tail = jnp.concatenate([r, rl, high, low, jnp.zeros((TAIL - 4, C), F32)], axis=0)
    return q, tail.astype(jnp.float16)


def decode(message):
    q, tail = message[:-TAIL].astype(F32), message[-TAIL:].astype(F32)
    r, rl = tail[0:1], tail[1:2]
    scale = r * r
    return q * scale, scale, (tail[2:3] + tail[3:4] * (1.0 / 1024.0)) * (rl * rl)


def ordered(own, got, place):
    out = jnp.zeros((len(got) + 1,) + own.shape, own.dtype)
    out = lax.dynamic_update_index_in_dim(out, own, place, 0)
    for d, g in enumerate(got, 1):
        out = lax.dynamic_update_index_in_dim(out, g, (place - d) % (len(got) + 1), 0)
    return out


def total(messages):
    parts = [decode(messages[k]) for k in range(messages.shape[0])]
    value, bound, loss = parts[0]
    for v, b, l in parts[1:]:
        value, bound, loss = value + v, bound + b, loss + l
    return value, bound, loss


def reduce_all(kept, sent, band, member):
    core = member % 2
    x, y = band % 4, band // 4 % 4
    z = 2 * (member // 2) + band // 16
    got = shift(sent, 4, 1)
    value = kept[:G] + got[:G]
    bound = kept[G : G + 1] + got[G : G + 1]
    loss = kept[G + 1 : G + 2] + got[G + 1 : G + 2]

    q, tail = encode(value, bound, loss)
    parts = q.reshape(4, G // 4, C)

    def part(k):
        return jnp.concatenate([lax.dynamic_index_in_dim(parts, k, 0, keepdims=False), tail], axis=0)

    got = [shift(part((x + d) % 4), 2, d) for d in range(1, 4)]
    value, bound, loss = total(ordered(part(x), got, x))

    message = jnp.concatenate(encode(value, bound, loss), axis=0)
    value, bound, loss = total(ordered(message, [shift(message, 1, d) for d in range(1, 4)], y))

    message = jnp.concatenate(encode(value, bound, loss), axis=0)
    value, bound, loss = total(ordered(message, [shift_z(message, d) for d in range(1, 4)], z))

    message = jnp.concatenate(encode(value, bound, loss), axis=0)
    messages = ordered(message, [shift(message, 2, d) for d in range(1, 4)], x)
    value = jnp.concatenate([decode(messages[k])[0] for k in range(4)], axis=0)
    other = shift(value, 4, 1)
    first = jnp.where(core == 0, value, other)
    second = jnp.where(core == 0, other, value)
    return loss[0, 0], first.reshape(3, 3, C, C), second.reshape(3, 3, C, C)


def chip_row(half, src, r, dst, sem):
    cut = LON - (HALF - LEFT)
    left = [
        pltpu.make_async_copy(src.at[r, pl.ds(LON - LEFT, LEFT)], dst.at[pl.ds(0, LEFT)], sem.at[0]),
        pltpu.make_async_copy(
            src.at[r, pl.ds(0, W - LEFT)], dst.at[pl.ds(LEFT, W - LEFT)], sem.at[1]
        ),
    ]
    right = [
        pltpu.make_async_copy(src.at[r, pl.ds(HALF - LEFT, cut)], dst.at[pl.ds(0, cut)], sem.at[0]),
        pltpu.make_async_copy(src.at[r, pl.ds(0, W - cut)], dst.at[pl.ds(cut, W - cut)], sem.at[1]),
    ]
    return [(half == 0, left), (half == 1, right)]


def own_window(quarter, src, dst, sem):
    cut = LON - (3 * OWN - LEFT)
    middle = pl.multiple_of(quarter * OWN - LEFT, 8)
    first = [
        pltpu.make_async_copy(
            src.at[:, pl.ds(LON - LEFT, LEFT)], dst.at[:, pl.ds(0, LEFT)], sem.at[0]
        ),
        pltpu.make_async_copy(
            src.at[:, pl.ds(0, J - LEFT)], dst.at[:, pl.ds(LEFT, J - LEFT)], sem.at[1]
        ),
    ]
    inner = [pltpu.make_async_copy(src.at[:, pl.ds(middle, J)], dst, sem.at[0])]
    last = [
        pltpu.make_async_copy(
            src.at[:, pl.ds(3 * OWN - LEFT, cut)], dst.at[:, pl.ds(0, cut)], sem.at[0]
        ),
        pltpu.make_async_copy(
            src.at[:, pl.ds(0, J - cut)], dst.at[:, pl.ds(cut, J - cut)], sem.at[1]
        ),
    ]
    return [(quarter == 0, first), ((quarter == 1) | (quarter == 2), inner), (quarter == 3, last)]


def start(cases):
    for cond, copies in cases:

        @pl.when(cond)
        def _():
            for c in copies:
                c.start()


def wait(cases):
    for cond, copies in cases:

        @pl.when(cond)
        def _():
            for c in copies:
                c.wait()


def edge_kernel(counts_ref, place_ref, state_ref, target_ref, one_ref, two_ref, three_ref, flag_ref, sem):
    band = place_ref[0]
    member = place_ref[1]
    half, core = member // 2, member % 2
    n = counts_ref[band]
    back = 2 * core - 1
    near = counts_ref[jnp.clip(band + back, 0, 31)]
    far = counts_ref[jnp.clip(band + 2 * back, 0, 31)]
    row = lambda k: jnp.where(core == 0, jnp.maximum(n - 1 - k, 0), k)
    sends = [(state_ref, 0, one_ref, 0), (state_ref, 1, one_ref, 1), (state_ref, 2, one_ref, 2)]
    sends += [(target_ref, 0, one_ref, 3)]
    sends += [(state_ref, 0, two_ref, 0), (state_ref, 1, two_ref, 1), (state_ref, 0, three_ref, 0)]
    cases = []
    for i, (src, k, dst, slot) in enumerate(sends):
        cases += chip_row(half, src, row(k), dst.at[slot], sem.at[i])
    start(cases)
    ones = jnp.ones((1, C), F32)
    flag_ref[0:1] = ones * (near >= 2).astype(F32)
    flag_ref[1:2] = ones * (near >= 3).astype(F32)
    flag_ref[2:3] = ones * (near == 2).astype(F32)
    flag_ref[3:4] = ones * (far >= 2).astype(F32)
    flag_ref[4:8] = jnp.zeros((4, C), F32)
    wait(cases)


def edges(counts, place, state, target):
    smem = pl.BlockSpec(memory_space=pltpu.SMEM)
    vmem = pl.BlockSpec(memory_space=pltpu.VMEM)
    hbm = pl.BlockSpec(memory_space=pl.ANY)
    rows = lambda k: jax.ShapeDtypeStruct((k, W, C), BF)
    return pl.pallas_call(
        edge_kernel,
        out_shape=(rows(4), rows(2), rows(1), jax.ShapeDtypeStruct((8, C), F32)),
        in_specs=[smem, smem, hbm, hbm],
        out_specs=(hbm, hbm, hbm, vmem),
        scratch_shapes=[pltpu.SemaphoreType.DMA((7, 2))],
        name="edge_rows",
    )(counts, place, state, target)


def kernel(
    counts_ref, seeds_ref, place_ref, weight_ref,
    state_ref, target_ref, mine_ref, other_ref,
    amp_ref, w1_ref, w2_ref, wt_ref,
    grads_ref, cells_ref,
    state_s, tgt_s, hash_s, bufs, cbuf_s, crps_s,
    in3, hid3, cot3_s, pre_s, fc_s, ya_s, yb_s, acc_s, acc2_s, sem,
):
    band = place_ref[0]
    quarter = place_ref[1]
    core = quarter % 2
    n = counts_ref[band]
    offset = lax.fori_loop(0, band, lambda b, s: s + counts_ref[b], jnp.int32(0))

    copies = own_window(quarter, state_ref, state_s.at[pl.ds(DEPTH, SLOTS)], sem.at[0])
    copies += own_window(quarter, target_ref, tgt_s.at[pl.ds(1, SLOTS)], sem.at[1])
    start(copies)

    for buf in bufs:
        buf[0:PAD] = jnp.zeros((PAD, C), F32)
        buf[PAD + J :] = jnp.zeros((PAD, C), F32)

    cols = lax.broadcasted_iota(jnp.int32, (J, C), 0)
    chan = lax.broadcasted_iota(jnp.int32, (J, C), 1)
    lon = quarter * OWN - LEFT + cols
    lon = jnp.where(lon < 0, lon + LON, jnp.where(lon >= LON, lon - LON, lon))
    hash_s[...] = lon * 668265263 + chan * 1274126177

    wait(copies)

    def put_edges(above, below):
        for slot, k in ((2, 0), (1, 1), (0, 2)):
            state_s[slot] = above[k]
        for slot, k in ((0, 0), (1, 1), (2, 2)):
            state_s[DEPTH + n + slot] = below[k]
        tgt_s[0] = above[3]
        tgt_s[1 + n] = below[3]

    @pl.when(core == 0)
    def _():
        put_edges(mine_ref, other_ref)

    @pl.when(core == 1)
    def _():
        put_edges(other_ref, mine_ref)

    def outside(e):
        g = offset - DEPTH + e
        return (g < 0) | (g >= ROWS_TOTAL)

    def trim(ref, m, slot):
        ref[m, slot, 0:LEFT] = jnp.zeros((LEFT, C), BF)
        ref[m, slot, LEFT + OWN :] = jnp.zeros((J - OWN - LEFT, C), BF)

    for e in (0, 1, 2):

        @pl.when(outside(e))
        def _():
            state_s[e] = jnp.zeros((J, C), BF)

    for e in range(DEPTH + 1, EXT):

        @pl.when(outside(e))
        def _():
            state_s[e] = jnp.zeros((J, C), BF)

    turn = [0]

    def put3(ref, m, slot, v):
        buf = bufs[turn[0] % len(bufs)]
        turn[0] += 1
        buf[PAD : PAD + J] = v
        ref[m, slot, :, C : 2 * C] = v.astype(BF)
        ref[m, slot, :, 0:C] = buf[PAD - 1 : PAD - 1 + J].astype(BF)
        ref[m, slot, :, 2 * C :] = buf[PAD + 1 : PAD + 1 + J].astype(BF)

    amp = amp_ref[...]
    amp_step = amp * (1.0 / 32768.0)
    amp_base = amp * (0.5 / 32768.0 - 1.0)

    def make_inputs(m, k):
        seed = seeds_ref[m] * 1103515245
        for j in range(2):
            e = 2 * k + j
            live = jnp.where(outside(e), 0.0, 1.0)
            h = hash_s[...] + ((offset - DEPTH + e) * 374761393 + seed)
            h = h ^ (h >> 13)
            h = h * 1274126177
            h = h ^ (h >> 16)
            v = (state_s[e].astype(F32) + amp_base * live) + (h & 65535).astype(F32) * (
                amp_step * live
            )
            put3(in3[k], m, j, v)

    def conv_pair(top, bottom, m, w):
        lhs = jnp.concatenate([top[m, 0], top[m, 1], bottom[m, 0], bottom[m, 1]], axis=1)
        return jnp.dot(lhs, w[...], preferred_element_type=F32)

    def make_hidden(m, p):
        out = conv_pair(in3[p], in3[p + 1], m, w1_ref)
        for j in range(2):
            e = 1 + 2 * p + j
            a = out[:, j * C : (j + 1) * C]
            if DEPTH <= e < DEPTH + SLOTS:
                pre_s[m, e - DEPTH] = a
            half = jnp.where(outside(e), 0.0, 0.5)
            put3(hid3[p], m, j, (a * half) * (1.0 + jnp.tanh(0.5 * a)))

    def make_forecast(m, p):
        out = conv_pair(hid3[p], hid3[p + 1], m, w2_ref)
        for j in range(2):
            v = in3[p + 1][m, j, :, C : 2 * C].astype(F32) + out[:, j * C : (j + 1) * C]
            fc_s[m, 2 * p + j] = v.astype(BF)

    def member(m, _):
        make_inputs(m, 0)
        make_inputs(m, 1)
        make_inputs(m, 2)
        make_hidden(m, 0)
        make_inputs(m, 3)
        make_hidden(m, 1)
        make_inputs(m, 4)
        make_forecast(m, 0)
        make_hidden(m, 2)
        make_forecast(m, 1)
        make_hidden(m, 3)
        make_forecast(m, 2)
        return 0

    lax.fori_loop(0, MEM, member, 0)

    pair_scale = 1.0 / (MEM * (MEM - 1))
    factor = 1.0 / math.sqrt(ROWS_TOTAL * LON)

    step = 32

    def crps_chunk(r, k, scale):
        at = pl.ds(k * step, step)
        if not isinstance(k, int):
            at = pl.ds(pl.multiple_of(k * step, step), step)
        t = tgt_s[r, at].astype(F32)
        f = [fc_s[m, r, at].astype(F32) for m in range(MEM)]
        skill = None
        spread = None
        slopes = []
        for m in range(MEM):
            d = f[m] - t
            q = d * d + SMOOTH
            inv = lax.rsqrt(q)
            skill = q * inv if skill is None else skill + q * inv
            slopes.append(d * inv * (MEM - 1.0))
        for a in range(MEM):
            for b in range(a + 1, MEM):
                d = f[a] - f[b]
                q = d * d + SMOOTH
                inv = lax.rsqrt(q)
                spread = q * inv if spread is None else spread + q * inv
                tilt = d * inv
                slopes[a] = slopes[a] - tilt
                slopes[b] = slopes[b] + tilt
        crps_s[at] = (skill * (MEM - 1.0) - spread) * pair_scale
        for m in range(MEM):
            start_at = PAD + k * step
            if not isinstance(k, int):
                start_at = pl.multiple_of(start_at, 8)
            cbuf_s[m, pl.ds(start_at, step)] = slopes[m] * scale

    def crps_weight(r):
        g = jnp.clip(offset - DEPTH + 2 + r, 0, ROWS_TOTAL - 1)
        return jnp.where(outside(r + 2), 0.0, weight_ref[g])

    def spread_out(r):
        for m in range(MEM):
            cot3_s[m, r, :, C : 2 * C] = cbuf_s[m, PAD : PAD + J].astype(BF)
            cot3_s[m, r, :, 0:C] = cbuf_s[m, PAD - 1 : PAD - 1 + J].astype(BF)
            cot3_s[m, r, :, 2 * C :] = cbuf_s[m, PAD + 1 : PAD + 1 + J].astype(BF)

    def keep_own(r, weight):
        for m in range(MEM):
            ya_s[m, r - 1] = jnp.where(r > n, 0.0, cbuf_s[m, PAD : PAD + J]).astype(BF)
            trim(ya_s, m, r - 1)
        mine = jnp.where(r > n, 0.0, weight * (1.0 / C))
        cells_ref[r - 1] = jnp.sum(jnp.transpose(crps_s[...]), axis=0, keepdims=True) * mine

    def crps_row(r):
        weight = crps_weight(r)
        for k in range(J // step):
            crps_chunk(r, k, weight * (factor * pair_scale))
        spread_out(r)
        if 1 <= r <= SLOTS:
            keep_own(r, weight)

    for m in range(MEM):
        cbuf_s[m, 0:PAD] = jnp.zeros((PAD, C), F32)
        cbuf_s[m, PAD + J :] = jnp.zeros((PAD, C), F32)

    def crps_looped(r, _):
        weight = crps_weight(r)

        def chunk(k, _):
            crps_chunk(r, k, weight * (factor * pair_scale))
            return 0

        lax.fori_loop(0, J // step, chunk, 0)
        spread_out(r)

        @pl.when(r >= 1)
        def _():
            keep_own(r, weight)

        return 0

    lax.fori_loop(0, 3, crps_looped, 0)

    def make_pre_cot(m, p):
        lhs = jnp.concatenate([cot3_s[m, 2 * p + r] for r in range(4)], axis=1)
        out = jnp.dot(lhs, wt_ref[...], preferred_element_type=F32)
        for k in range(2):
            s = 2 * p + k
            a = pre_s[m, s]
            t = jnp.tanh(0.5 * a)
            mine = jnp.where(s < n, 0.25, 0.0)
            v = out[:, k * C : (k + 1) * C] * (((1.0 + t) * mine) * (2.0 + a * (1.0 - t)))
            yb_s[m, s] = v.astype(BF)
            trim(yb_s, m, s)

    hidden_rows = [(hid3[(e - 1) // 2], (e - 1) % 2) for e in range(2, 8)]

    def grad_two(p):
        for g in (0, 2):
            ys = jnp.concatenate(
                [jnp.concatenate([ya_s[m, 2 * p], ya_s[m, 2 * p + 1]], axis=1) for m in (g, g + 1)],
                axis=0,
            )
            xs = jnp.concatenate(
                [
                    jnp.concatenate([ref[m, j] for ref, j in hidden_rows[2 * p : 2 * p + 4]], axis=1)
                    for m in (g, g + 1)
                ],
                axis=0,
            )
            part = lax.dot_general(ys, xs, (((0,), (0,)), ((), ())), preferred_element_type=F32)
            if p == 0 and g == 0:
                acc2_s[...] = part
            else:
                acc2_s[...] += part

    crps_row(3)
    grad_two(0)
    crps_row(4)
    for m in range(MEM):
        make_pre_cot(m, 0)
    crps_row(5)
    grad_two(1)
    for m in range(MEM):
        make_pre_cot(m, 1)
    loss = cells_ref[0] + cells_ref[1] + cells_ref[2] + cells_ref[3]
    lane = lax.broadcasted_iota(jnp.int32, (1, J), 1)
    loss = jnp.where((lane >= LEFT) & (lane < LEFT + OWN), loss, 0.0)

    def accumulate(rows, y):
        acc_s[...] = jnp.zeros_like(acc_s)

        def step(m, _):
            ys = jnp.concatenate(
                [
                    jnp.concatenate([y[m, 0], y[m, 1]], axis=1),
                    jnp.concatenate([y[m, 2], y[m, 3]], axis=1),
                ],
                axis=0,
            )
            xs = jnp.concatenate(
                [
                    jnp.concatenate([ref[m, j] for ref, j in rows[a : a + 4]], axis=1)
                    for a in (0, 2)
                ],
                axis=0,
            )
            acc_s[...] += lax.dot_general(
                ys, xs, (((0,), (0,)), ((), ())), preferred_element_type=F32
            )
            return 0

        lax.fori_loop(0, MEM, step, 0)

    def finish(acc, slot):
        biggest = jnp.zeros((C, C), F32)
        for k in range(9):
            blk = acc[0:C, k * C : (k + 1) * C] + acc[C:, 384 + k * C : 384 + (k + 1) * C]
            biggest = jnp.maximum(biggest, jnp.abs(blk))
            grads_ref[slot, k * C : (k + 1) * C] = jnp.transpose(blk)
        return biggest

    top2 = finish(acc2_s, 1 - core)
    accumulate([(in3[e // 2], e % 2) for e in range(2, 8)], yb_s)
    top1 = finish(acc_s, core)
    biggest = jnp.max(jnp.max(jnp.maximum(top1, top2), axis=0, keepdims=True), axis=1, keepdims=True)
    loss = jnp.sum(loss, axis=1, keepdims=True) * (1.0 / (ROWS_TOTAL * LON))
    for slot in range(2):
        grads_ref[slot, G : G + 1] = jnp.broadcast_to(biggest, (1, C))
        grads_ref[slot, G + 1 : G + 2] = jnp.broadcast_to(loss, (1, C))
        grads_ref[slot, G + 2 :] = jnp.zeros((6, C), F32)


def local_step(counts, seeds, place, weights, state, target, mine, other, amp, w1, w2, wt):
    smem = pl.BlockSpec(memory_space=pltpu.SMEM)
    vmem = pl.BlockSpec(memory_space=pltpu.VMEM)
    hbm = pl.BlockSpec(memory_space=pl.ANY)
    return pl.pallas_call(
        kernel,
        out_shape=(
            jax.ShapeDtypeStruct((2, G + 8, C), F32),
            jax.ShapeDtypeStruct((SLOTS, 1, J), F32),
        ),
        in_specs=[smem] * 4 + [hbm] * 2 + [vmem] * 6,
        out_specs=(vmem, vmem),
        scratch_shapes=[
            pltpu.VMEM((EXT, J, C), BF),
            pltpu.VMEM((SLOTS + 2, J, C), BF),
            pltpu.VMEM((J, C), jnp.int32),
            [pltpu.VMEM((J + 2 * PAD, C), F32) for _ in range(6)],
            pltpu.VMEM((MEM, J + 2 * PAD, C), F32),
            pltpu.VMEM((J, C), F32),
            [pltpu.VMEM((MEM, 2, J, 3 * C), BF) for _ in range(5)],
            [pltpu.VMEM((MEM, 2, J, 3 * C), BF) for _ in range(4)],
            pltpu.VMEM((MEM, EXT - 4, J, 3 * C), BF),
            pltpu.VMEM((MEM, SLOTS, J, C), F32),
            pltpu.VMEM((MEM, EXT - 4, J, C), BF),
            pltpu.VMEM((MEM, SLOTS, J, C), BF),
            pltpu.VMEM((MEM, SLOTS, J, C), BF),
            pltpu.VMEM((2 * C, 4 * 384), F32),
            pltpu.VMEM((2 * C, 4 * 384), F32),
            pltpu.SemaphoreType.DMA((2, 2)),
        ],
        compiler_params=pltpu.CompilerParams(vmem_limit_bytes=60 * 1024 * 1024),
        name="ensemble_step",
    )(counts, seeds, place, weights, state, target, mine, other, amp, w1, w2, wt)


def paired(filt):
    flat = filt.reshape(9 * C, C)
    return jnp.concatenate(
        [jnp.pad(flat, ((0, 3 * C), (0, 0))), jnp.pad(flat, ((3 * C, 0), (0, 0)))], axis=1
    )


def body(state, target, amp, filt1, filt2, counts, seed):
    band = lax.axis_index("band")
    member = lax.axis_index("member")
    core = member % 2
    weights = jnp.asarray(
        np.cos(np.pi * ((np.arange(ROWS_TOTAL) + 0.5) / GRID_ROWS - 0.5)).astype(np.float32)
    )
    place = jnp.stack([band, member]).astype(jnp.int32)
    seeds = jnp.where(jnp.arange(MEM) == member, seed, 0)
    seeds = seeds + shift(seeds, 4, 1)
    one, two, three, flags = edges(counts, place, state, target)

    def send(value, by):
        pairs = [(i, (i // 4 + by * (1 - 2 * (i % 2))) % 32 * 4 + i % 4) for i in range(128)]
        return lax.ppermute(value, BM, pairs)

    def flag(k):
        return flags[k : k + 1][None] > 0.5

    one, seeds = lax.optimization_barrier((one, seeds))
    g1 = send(one, 1)
    seeds = seeds + shift(seeds, 3, 1)
    two, three, seeds, filt1, filt2 = lax.optimization_barrier((two, three, seeds, filt1, filt2))
    g2 = send(two, 2)
    g3 = send(three, 3)
    w1 = paired(filt1)
    w2 = paired(filt2)
    wt = paired(jnp.transpose(filt2[::-1, ::-1], (0, 1, 3, 2)))
    g3, w1, w2, wt = lax.optimization_barrier((g3, w1, w2, wt))
    row2 = jnp.where(flag(0), g1[1:2], g2[:1])
    row3 = jnp.where(
        flag(1), g1[2:3], jnp.where(flag(2), g2[:1], jnp.where(flag(3), g2[1:], g3))
    )
    halo = jnp.concatenate([g1[:1], row2, row3, g1[3:]], axis=0)
    mine = lax.dynamic_slice_in_dim(halo, OWN * core, J, 1)
    other = shift(lax.dynamic_slice_in_dim(halo, OWN * (1 - core), J, 1), 4, 1)

    grads, cells = local_step(
        counts, seeds, place, weights, state, target, mine, other, amp[None], w1, w2, wt
    )

    mean_loss, grad_one, grad_two = reduce_all(grads[0], grads[1], band, member)
    return cells[:, 0, LEFT : LEFT + OWN], mean_loss, grad_one, grad_two


def solution(mesh):
    in_specs = (P("band", None, None), P("band", None, None), P(), P(), P(), P(), P("member"))
    out_specs = (P("band", "member"), P(), P(), P())
    return jax.shard_map(body, mesh=mesh, in_specs=in_specs, out_specs=out_specs, check_vma=False)
```

```python
import math

import jax
import jax.numpy as jnp
import numpy as np
from jax import lax
from jax.experimental import pallas as pl
from jax.experimental.pallas import tpu as pltpu
from jax.sharding import PartitionSpec as P

GRID_ROWS = 721
HALF = 720
ROWS_TOTAL = 96
SMOOTH = 0.01
LON = 1440
OWN = 360
LEFT = 8
J = 384
C = 128
MEM = 4
SLOTS = 4
DEPTH = 3
EXT = SLOTS + 2 * DEPTH
PAD = 8
W = 752
G = 1152
TAIL = 16
BF = jnp.bfloat16
F32 = jnp.float32
BM = ("band", "member")


def coords(i):
    return [i // 64, i // 16 % 4, i // 4 % 4, i // 2 % 2, i % 2]


def index(v):
    return (((v[0] * 4 + v[1]) * 4 + v[2]) * 2 + v[3]) * 2 + v[4]


SIZES = [2, 4, 4, 2, 2]


def permute(value, move):
    return lax.ppermute(value, BM, [(i, index(move(coords(i)))) for i in range(128)])


def shift(value, dim, by):
    def move(v):
        v[dim] = (v[dim] + by) % SIZES[dim]
        return v

    return permute(value, move)


def shift_z(value, by):
    def move(v):
        z = (2 * v[3] + v[0] + by) % 4
        v[3], v[0] = z // 2, z % 2
        return v

    return permute(value, move)


def root(bound):
    return half(jnp.sqrt(jnp.maximum(bound, 2.0**-24)) * 1.001)


def half(value):
    return lax.reduce_precision(value, exponent_bits=5, mantissa_bits=10)


def encode(value, bound, loss):
    r = root(bound)
    q = (value * (1.0 / (r * r))).astype(jnp.float16)
    rl = root(jnp.abs(loss))
    share = loss * (1.0 / (rl * rl))
    high = half(share)
    low = (share - high) * 1024.0
    tail = jnp.concatenate([r, rl, high, low, jnp.zeros((TAIL - 4, C), F32)], axis=0)
    return q, tail.astype(jnp.float16)


def decode(message):
    q, tail = message[:-TAIL].astype(F32), message[-TAIL:].astype(F32)
    r, rl = tail[0:1], tail[1:2]
    scale = r * r
    return q * scale, scale, (tail[2:3] + tail[3:4] * (1.0 / 1024.0)) * (rl * rl)


def ordered(own, got, place):
    out = jnp.zeros((len(got) + 1,) + own.shape, own.dtype)
    out = lax.dynamic_update_index_in_dim(out, own, place, 0)
    for d, g in enumerate(got, 1):
        out = lax.dynamic_update_index_in_dim(out, g, (place - d) % (len(got) + 1), 0)
    return out


def total(messages):
    parts = [decode(messages[k]) for k in range(messages.shape[0])]
    value, bound, loss = parts[0]
    for v, b, l in parts[1:]:
        value, bound, loss = value + v, bound + b, loss + l
    return value, bound, loss


def reduce_all(kept, sent, band, member):
    core = member % 2
    x, y = band % 4, band // 4 % 4
    z = 2 * (member // 2) + band // 16
    got = shift(sent, 4, 1)
    value = kept[:G] + got[:G]
    bound = kept[G : G + 1] + got[G : G + 1]
    loss = kept[G + 1 : G + 2] + got[G + 1 : G + 2]

    q, tail = encode(value, bound, loss)
    parts = q.reshape(4, G // 4, C)

    def part(k):
        return jnp.concatenate([lax.dynamic_index_in_dim(parts, k, 0, keepdims=False), tail], axis=0)

    got = [shift(part((x + d) % 4), 2, d) for d in range(1, 4)]
    value, bound, loss = total(ordered(part(x), got, x))

    message = jnp.concatenate(encode(value, bound, loss), axis=0)
    value, bound, loss = total(ordered(message, [shift(message, 1, d) for d in range(1, 4)], y))

    message = jnp.concatenate(encode(value, bound, loss), axis=0)
    value, bound, loss = total(ordered(message, [shift_z(message, d) for d in range(1, 4)], z))

    message = jnp.concatenate(encode(value, bound, loss), axis=0)
    messages = ordered(message, [shift(message, 2, d) for d in range(1, 4)], x)
    value = jnp.concatenate([decode(messages[k])[0] for k in range(4)], axis=0)
    other = shift(value, 4, 1)
    first = jnp.where(core == 0, value, other)
    second = jnp.where(core == 0, other, value)
    return loss[0, 0], first.reshape(3, 3, C, C), second.reshape(3, 3, C, C)


def chip_row(half, src, r, dst, sem):
    cut = LON - (HALF - LEFT)
    left = [
        pltpu.make_async_copy(src.at[r, pl.ds(LON - LEFT, LEFT)], dst.at[pl.ds(0, LEFT)], sem.at[0]),
        pltpu.make_async_copy(
            src.at[r, pl.ds(0, W - LEFT)], dst.at[pl.ds(LEFT, W - LEFT)], sem.at[1]
        ),
    ]
    right = [
        pltpu.make_async_copy(src.at[r, pl.ds(HALF - LEFT, cut)], dst.at[pl.ds(0, cut)], sem.at[0]),
        pltpu.make_async_copy(src.at[r, pl.ds(0, W - cut)], dst.at[pl.ds(cut, W - cut)], sem.at[1]),
    ]
    return [(half == 0, left), (half == 1, right)]


def own_window(quarter, src, dst, sem):
    cut = LON - (3 * OWN - LEFT)
    middle = pl.multiple_of(quarter * OWN - LEFT, 8)
    first = [
        pltpu.make_async_copy(
            src.at[:, pl.ds(LON - LEFT, LEFT)], dst.at[:, pl.ds(0, LEFT)], sem.at[0]
        ),
        pltpu.make_async_copy(
            src.at[:, pl.ds(0, J - LEFT)], dst.at[:, pl.ds(LEFT, J - LEFT)], sem.at[1]
        ),
    ]
    inner = [pltpu.make_async_copy(src.at[:, pl.ds(middle, J)], dst, sem.at[0])]
    last = [
        pltpu.make_async_copy(
            src.at[:, pl.ds(3 * OWN - LEFT, cut)], dst.at[:, pl.ds(0, cut)], sem.at[0]
        ),
        pltpu.make_async_copy(
            src.at[:, pl.ds(0, J - cut)], dst.at[:, pl.ds(cut, J - cut)], sem.at[1]
        ),
    ]
    return [(quarter == 0, first), ((quarter == 1) | (quarter == 2), inner), (quarter == 3, last)]


def start(cases):
    for cond, copies in cases:

        @pl.when(cond)
        def _():
            for c in copies:
                c.start()


def wait(cases):
    for cond, copies in cases:

        @pl.when(cond)
        def _():
            for c in copies:
                c.wait()


def edge_kernel(counts_ref, place_ref, state_ref, target_ref, one_ref, two_ref, three_ref, flag_ref, sem):
    band = place_ref[0]
    member = place_ref[1]
    half, core = member // 2, member % 2
    n = counts_ref[band]
    back = 2 * core - 1
    near = counts_ref[jnp.clip(band + back, 0, 31)]
    far = counts_ref[jnp.clip(band + 2 * back, 0, 31)]
    row = lambda k: jnp.where(core == 0, jnp.maximum(n - 1 - k, 0), k)
    sends = [(state_ref, 0, one_ref, 0), (state_ref, 1, one_ref, 1), (state_ref, 2, one_ref, 2)]
    sends += [(target_ref, 0, one_ref, 3)]
    sends += [(state_ref, 0, two_ref, 0), (state_ref, 1, two_ref, 1), (state_ref, 0, three_ref, 0)]
    cases = []
    for i, (src, k, dst, slot) in enumerate(sends):
        cases += chip_row(half, src, row(k), dst.at[slot], sem.at[i])
    start(cases)
    ones = jnp.ones((1, C), F32)
    flag_ref[0:1] = ones * (near >= 2).astype(F32)
    flag_ref[1:2] = ones * (near >= 3).astype(F32)
    flag_ref[2:3] = ones * (near == 2).astype(F32)
    flag_ref[3:4] = ones * (far >= 2).astype(F32)
    flag_ref[4:8] = jnp.zeros((4, C), F32)
    wait(cases)


def edges(counts, place, state, target):
    smem = pl.BlockSpec(memory_space=pltpu.SMEM)
    vmem = pl.BlockSpec(memory_space=pltpu.VMEM)
    hbm = pl.BlockSpec(memory_space=pl.ANY)
    rows = lambda k: jax.ShapeDtypeStruct((k, W, C), BF)
    return pl.pallas_call(
        edge_kernel,
        out_shape=(rows(4), rows(2), rows(1), jax.ShapeDtypeStruct((8, C), F32)),
        in_specs=[smem, smem, hbm, hbm],
        out_specs=(vmem,) * 4,
        scratch_shapes=[pltpu.SemaphoreType.DMA((7, 2))],
        name="edge_rows",
    )(counts, place, state, target)


def kernel(
    counts_ref, seeds_ref, place_ref, weight_ref,
    state_ref, target_ref, mine_ref, other_ref,
    amp_ref, w1_ref, w2_ref, wt_ref,
    grads_ref, cells_ref,
    state_s, tgt_s, hash_s, bufs, cbuf_s, crps_s,
    in3, hid3, cot3_s, pre_s, fc_s, ya_s, yb_s, acc_s, acc2_s, sem,
):
    band = place_ref[0]
    quarter = place_ref[1]
    core = quarter % 2
    n = counts_ref[band]
    offset = lax.fori_loop(0, band, lambda b, s: s + counts_ref[b], jnp.int32(0))

    copies = own_window(quarter, state_ref, state_s.at[pl.ds(DEPTH, SLOTS)], sem.at[0])
    copies += own_window(quarter, target_ref, tgt_s.at[pl.ds(1, SLOTS)], sem.at[1])
    start(copies)

    for buf in bufs:
        buf[0:PAD] = jnp.zeros((PAD, C), F32)
        buf[PAD + J :] = jnp.zeros((PAD, C), F32)

    cols = lax.broadcasted_iota(jnp.int32, (J, C), 0)
    chan = lax.broadcasted_iota(jnp.int32, (J, C), 1)
    lon = quarter * OWN - LEFT + cols
    lon = jnp.where(lon < 0, lon + LON, jnp.where(lon >= LON, lon - LON, lon))
    hash_s[...] = lon * 668265263 + chan * 1274126177

    wait(copies)

    def put_edges(above, below):
        for slot, k in ((2, 0), (1, 1), (0, 2)):
            state_s[slot] = above[k]
        for slot, k in ((0, 0), (1, 1), (2, 2)):
            state_s[DEPTH + n + slot] = below[k]
        tgt_s[0] = above[3]
        tgt_s[1 + n] = below[3]

    @pl.when(core == 0)
    def _():
        put_edges(mine_ref, other_ref)

    @pl.when(core == 1)
    def _():
        put_edges(other_ref, mine_ref)

    def outside(e):
        g = offset - DEPTH + e
        return (g < 0) | (g >= ROWS_TOTAL)

    def trim(ref, m, slot):
        ref[m, slot, 0:LEFT] = jnp.zeros((LEFT, C), BF)
        ref[m, slot, LEFT + OWN :] = jnp.zeros((J - OWN - LEFT, C), BF)

    for e in (0, 1, 2):

        @pl.when(outside(e))
        def _():
            state_s[e] = jnp.zeros((J, C), BF)

    for e in range(DEPTH + 1, EXT):

        @pl.when(outside(e))
        def _():
            state_s[e] = jnp.zeros((J, C), BF)

    turn = [0]

    def put3(ref, m, slot, v):
        buf = bufs[turn[0] % len(bufs)]
        turn[0] += 1
        buf[PAD : PAD + J] = v
        ref[m, slot, :, C : 2 * C] = v.astype(BF)
        ref[m, slot, :, 0:C] = buf[PAD - 1 : PAD - 1 + J].astype(BF)
        ref[m, slot, :, 2 * C :] = buf[PAD + 1 : PAD + 1 + J].astype(BF)

    amp = amp_ref[...]
    amp_step = amp * (1.0 / 32768.0)
    amp_base = amp * (0.5 / 32768.0 - 1.0)

    def make_inputs(m, k):
        seed = seeds_ref[m] * 1103515245
        for j in range(2):
            e = 2 * k + j
            live = jnp.where(outside(e), 0.0, 1.0)
            h = hash_s[...] + ((offset - DEPTH + e) * 374761393 + seed)
            h = h ^ (h >> 13)
            h = h * 1274126177
            h = h ^ (h >> 16)
            v = (state_s[e].astype(F32) + amp_base * live) + (h & 65535).astype(F32) * (
                amp_step * live
            )
            put3(in3[k], m, j, v)

    def conv_pair(top, bottom, m, w):
        lhs = jnp.concatenate([top[m, 0], top[m, 1], bottom[m, 0], bottom[m, 1]], axis=1)
        return jnp.dot(lhs, w[...], preferred_element_type=F32)

    def make_hidden(m, p):
        out = conv_pair(in3[p], in3[p + 1], m, w1_ref)
        for j in range(2):
            e = 1 + 2 * p + j
            a = out[:, j * C : (j + 1) * C]
            if DEPTH <= e < DEPTH + SLOTS:
                pre_s[m, e - DEPTH] = a
            half = jnp.where(outside(e), 0.0, 0.5)
            put3(hid3[p], m, j, (a * half) * (1.0 + jnp.tanh(0.5 * a)))

    def make_forecast(m, p):
        out = conv_pair(hid3[p], hid3[p + 1], m, w2_ref)
        for j in range(2):
            v = in3[p + 1][m, j, :, C : 2 * C].astype(F32) + out[:, j * C : (j + 1) * C]
            fc_s[m, 2 * p + j] = v.astype(BF)

    def member(m, _):
        make_inputs(m, 0)
        make_inputs(m, 1)
        make_inputs(m, 2)
        make_hidden(m, 0)
        make_inputs(m, 3)
        make_hidden(m, 1)
        make_inputs(m, 4)
        make_forecast(m, 0)
        make_hidden(m, 2)
        make_forecast(m, 1)
        make_hidden(m, 3)
        make_forecast(m, 2)
        return 0

    lax.fori_loop(0, MEM, member, 0)

    pair_scale = 1.0 / (MEM * (MEM - 1))
    factor = 1.0 / math.sqrt(ROWS_TOTAL * LON)

    step = 32

    def crps_chunk(r, k, scale):
        at = pl.ds(k * step, step)
        if not isinstance(k, int):
            at = pl.ds(pl.multiple_of(k * step, step), step)
        t = tgt_s[r, at].astype(F32)
        f = [fc_s[m, r, at].astype(F32) for m in range(MEM)]
        skill = None
        spread = None
        slopes = []
        for m in range(MEM):
            d = f[m] - t
            q = d * d + SMOOTH
            inv = lax.rsqrt(q)
            skill = q * inv if skill is None else skill + q * inv
            slopes.append(d * inv * (MEM - 1.0))
        for a in range(MEM):
            for b in range(a + 1, MEM):
                d = f[a] - f[b]
                q = d * d + SMOOTH
                inv = lax.rsqrt(q)
                spread = q * inv if spread is None else spread + q * inv
                tilt = d * inv
                slopes[a] = slopes[a] - tilt
                slopes[b] = slopes[b] + tilt
        crps_s[at] = (skill * (MEM - 1.0) - spread) * pair_scale
        for m in range(MEM):
            start_at = PAD + k * step
            if not isinstance(k, int):
                start_at = pl.multiple_of(start_at, 8)
            cbuf_s[m, pl.ds(start_at, step)] = slopes[m] * scale

    def crps_weight(r):
        g = jnp.clip(offset - DEPTH + 2 + r, 0, ROWS_TOTAL - 1)
        return jnp.where(outside(r + 2), 0.0, weight_ref[g])

    def spread_out(r):
        for m in range(MEM):
            cot3_s[m, r, :, C : 2 * C] = cbuf_s[m, PAD : PAD + J].astype(BF)
            cot3_s[m, r, :, 0:C] = cbuf_s[m, PAD - 1 : PAD - 1 + J].astype(BF)
            cot3_s[m, r, :, 2 * C :] = cbuf_s[m, PAD + 1 : PAD + 1 + J].astype(BF)

    def keep_own(r, weight):
        for m in range(MEM):
            ya_s[m, r - 1] = jnp.where(r > n, 0.0, cbuf_s[m, PAD : PAD + J]).astype(BF)
            trim(ya_s, m, r - 1)
        mine = jnp.where(r > n, 0.0, weight * (1.0 / C))
        cells_ref[r - 1] = jnp.sum(jnp.transpose(crps_s[...]), axis=0, keepdims=True) * mine

    def crps_row(r):
        weight = crps_weight(r)
        for k in range(J // step):
            crps_chunk(r, k, weight * (factor * pair_scale))
        spread_out(r)
        if 1 <= r <= SLOTS:
            keep_own(r, weight)

    for m in range(MEM):
        cbuf_s[m, 0:PAD] = jnp.zeros((PAD, C), F32)
        cbuf_s[m, PAD + J :] = jnp.zeros((PAD, C), F32)

    def crps_looped(r, _):
        weight = crps_weight(r)

        def chunk(k, _):
            crps_chunk(r, k, weight * (factor * pair_scale))
            return 0

        lax.fori_loop(0, J // step, chunk, 0)
        spread_out(r)

        @pl.when(r >= 1)
        def _():
            keep_own(r, weight)

        return 0

    lax.fori_loop(0, 3, crps_looped, 0)

    def make_pre_cot(m, p):
        lhs = jnp.concatenate([cot3_s[m, 2 * p + r] for r in range(4)], axis=1)
        out = jnp.dot(lhs, wt_ref[...], preferred_element_type=F32)
        for k in range(2):
            s = 2 * p + k
            a = pre_s[m, s]
            t = jnp.tanh(0.5 * a)
            mine = jnp.where(s < n, 0.25, 0.0)
            v = out[:, k * C : (k + 1) * C] * (((1.0 + t) * mine) * (2.0 + a * (1.0 - t)))
            yb_s[m, s] = v.astype(BF)
            trim(yb_s, m, s)

    hidden_rows = [(hid3[(e - 1) // 2], (e - 1) % 2) for e in range(2, 8)]

    def grad_two(p):
        for g in (0, 2):
            ys = jnp.concatenate(
                [jnp.concatenate([ya_s[m, 2 * p], ya_s[m, 2 * p + 1]], axis=1) for m in (g, g + 1)],
                axis=0,
            )
            xs = jnp.concatenate(
                [
                    jnp.concatenate([ref[m, j] for ref, j in hidden_rows[2 * p : 2 * p + 4]], axis=1)
                    for m in (g, g + 1)
                ],
                axis=0,
            )
            part = lax.dot_general(ys, xs, (((0,), (0,)), ((), ())), preferred_element_type=F32)
            if p == 0 and g == 0:
                acc2_s[...] = part
            else:
                acc2_s[...] += part

    crps_row(3)
    grad_two(0)
    crps_row(4)
    for m in range(MEM):
        make_pre_cot(m, 0)
    crps_row(5)
    grad_two(1)
    for m in range(MEM):
        make_pre_cot(m, 1)
    loss = cells_ref[0] + cells_ref[1] + cells_ref[2] + cells_ref[3]
    lane = lax.broadcasted_iota(jnp.int32, (1, J), 1)
    loss = jnp.where((lane >= LEFT) & (lane < LEFT + OWN), loss, 0.0)

    def accumulate(rows, y):
        acc_s[...] = jnp.zeros_like(acc_s)

        def step(m, _):
            ys = jnp.concatenate(
                [
                    jnp.concatenate([y[m, 0], y[m, 1]], axis=1),
                    jnp.concatenate([y[m, 2], y[m, 3]], axis=1),
                ],
                axis=0,
            )
            xs = jnp.concatenate(
                [
                    jnp.concatenate([ref[m, j] for ref, j in rows[a : a + 4]], axis=1)
                    for a in (0, 2)
                ],
                axis=0,
            )
            acc_s[...] += lax.dot_general(
                ys, xs, (((0,), (0,)), ((), ())), preferred_element_type=F32
            )
            return 0

        lax.fori_loop(0, MEM, step, 0)

    def finish(acc, slot):
        biggest = jnp.zeros((C, C), F32)
        for k in range(9):
            blk = acc[0:C, k * C : (k + 1) * C] + acc[C:, 384 + k * C : 384 + (k + 1) * C]
            biggest = jnp.maximum(biggest, jnp.abs(blk))
            grads_ref[slot, k * C : (k + 1) * C] = jnp.transpose(blk)
        return biggest

    top2 = finish(acc2_s, 1 - core)
    accumulate([(in3[e // 2], e % 2) for e in range(2, 8)], yb_s)
    top1 = finish(acc_s, core)
    biggest = jnp.max(jnp.max(jnp.maximum(top1, top2), axis=0, keepdims=True), axis=1, keepdims=True)
    loss = jnp.sum(loss, axis=1, keepdims=True) * (1.0 / (ROWS_TOTAL * LON))
    for slot in range(2):
        grads_ref[slot, G : G + 1] = jnp.broadcast_to(biggest, (1, C))
        grads_ref[slot, G + 1 : G + 2] = jnp.broadcast_to(loss, (1, C))
        grads_ref[slot, G + 2 :] = jnp.zeros((6, C), F32)


def local_step(counts, seeds, place, weights, state, target, mine, other, amp, w1, w2, wt):
    smem = pl.BlockSpec(memory_space=pltpu.SMEM)
    vmem = pl.BlockSpec(memory_space=pltpu.VMEM)
    hbm = pl.BlockSpec(memory_space=pl.ANY)
    return pl.pallas_call(
        kernel,
        out_shape=(
            jax.ShapeDtypeStruct((2, G + 8, C), F32),
            jax.ShapeDtypeStruct((SLOTS, 1, J), F32),
        ),
        in_specs=[smem] * 4 + [hbm] * 2 + [vmem] * 6,
        out_specs=(vmem, vmem),
        scratch_shapes=[
            pltpu.VMEM((EXT, J, C), BF),
            pltpu.VMEM((SLOTS + 2, J, C), BF),
            pltpu.VMEM((J, C), jnp.int32),
            [pltpu.VMEM((J + 2 * PAD, C), F32) for _ in range(6)],
            pltpu.VMEM((MEM, J + 2 * PAD, C), F32),
            pltpu.VMEM((J, C), F32),
            [pltpu.VMEM((MEM, 2, J, 3 * C), BF) for _ in range(5)],
            [pltpu.VMEM((MEM, 2, J, 3 * C), BF) for _ in range(4)],
            pltpu.VMEM((MEM, EXT - 4, J, 3 * C), BF),
            pltpu.VMEM((MEM, SLOTS, J, C), F32),
            pltpu.VMEM((MEM, EXT - 4, J, C), BF),
            pltpu.VMEM((MEM, SLOTS, J, C), BF),
            pltpu.VMEM((MEM, SLOTS, J, C), BF),
            pltpu.VMEM((2 * C, 4 * 384), F32),
            pltpu.VMEM((2 * C, 4 * 384), F32),
            pltpu.SemaphoreType.DMA((2, 2)),
        ],
        compiler_params=pltpu.CompilerParams(vmem_limit_bytes=60 * 1024 * 1024),
        name="ensemble_step",
    )(counts, seeds, place, weights, state, target, mine, other, amp, w1, w2, wt)


def paired(filt):
    flat = filt.reshape(9 * C, C)
    return jnp.concatenate(
        [jnp.pad(flat, ((0, 3 * C), (0, 0))), jnp.pad(flat, ((3 * C, 0), (0, 0)))], axis=1
    )


def body(state, target, amp, filt1, filt2, counts, seed):
    band = lax.axis_index("band")
    member = lax.axis_index("member")
    core = member % 2
    weights = jnp.asarray(
        np.cos(np.pi * ((np.arange(ROWS_TOTAL) + 0.5) / GRID_ROWS - 0.5)).astype(np.float32)
    )
    place = jnp.stack([band, member]).astype(jnp.int32)
    seeds = jnp.where(jnp.arange(MEM) == member, seed, 0)
    seeds = seeds + shift(seeds, 4, 1)
    one, two, three, flags = edges(counts, place, state, target)

    def send(value, by):
        pairs = [(i, (i // 4 + by * (1 - 2 * (i % 2))) % 32 * 4 + i % 4) for i in range(128)]
        return lax.ppermute(value, BM, pairs)

    def flag(k):
        return flags[k : k + 1][None] > 0.5

    one, seeds = lax.optimization_barrier((one, seeds))
    g1 = send(one, 1)
    seeds = seeds + shift(seeds, 3, 1)
    two, three, seeds, filt1, filt2 = lax.optimization_barrier((two, three, seeds, filt1, filt2))
    g2 = send(two, 2)
    g3 = send(three, 3)
    w1 = paired(filt1)
    w2 = paired(filt2)
    wt = paired(jnp.transpose(filt2[::-1, ::-1], (0, 1, 3, 2)))
    g3, w1, w2, wt = lax.optimization_barrier((g3, w1, w2, wt))
    row2 = jnp.where(flag(0), g1[1:2], g2[:1])
    row3 = jnp.where(
        flag(1), g1[2:3], jnp.where(flag(2), g2[:1], jnp.where(flag(3), g2[1:], g3))
    )
    halo = jnp.concatenate([g1[:1], row2, row3, g1[3:]], axis=0)
    mine = lax.dynamic_slice_in_dim(halo, OWN * core, J, 1)
    other = shift(lax.dynamic_slice_in_dim(halo, OWN * (1 - core), J, 1), 4, 1)

    grads, cells = local_step(
        counts, seeds, place, weights, state, target, mine, other, amp[None], w1, w2, wt
    )

    mean_loss, grad_one, grad_two = reduce_all(grads[0], grads[1], band, member)
    return cells[:, 0, LEFT : LEFT + OWN], mean_loss, grad_one, grad_two


def solution(mesh):
    in_specs = (P("band", None, None), P("band", None, None), P(), P(), P(), P(), P("member"))
    out_specs = (P("band", "member"), P(), P(), P())
    return jax.shard_map(body, mesh=mesh, in_specs=in_specs, out_specs=out_specs, check_vma=False)
```
